512 devices in a mesh: dp: 8 (over y, core), seq: 64 (over x, z).
Axes of the slice: x: 4, y: 4, z: 16, core: 2. Of those that a mesh axis runs over, the one named last changes fastest.
Arguments:
- queries: bfloat16 [16384, 3072], P('seq', 'dp'), may hold values from -6 to 6
- keys: bfloat16 [16384, 3072], P('seq', 'dp'), may hold values from -6 to 6
- values: bfloat16 [16384, 3072], P('seq', 'dp'), may hold values from -6 to 6
- out_grad: bfloat16 [16384, 3072], P('seq', 'dp'), may hold values from -6 to 6
- log_decay: float32 [16384, 24], P('seq', 'dp'), may hold values from -0.61 to 0
- norm_gain: float32 [3072], P('dp'), may hold values from 0.1 to 1.9
- doc_ids: int32 [128], P('seq'), may hold values from 0 to 3, never falling along the last dimension, each value on 1 to 64 neighbouring positions
Outputs:
- key_grad: bfloat16 [16384, 3072], P('seq', 'dp')
- value_grad: bfloat16 [16384, 3072], P('seq', 'dp')
- gain_grad: float32 [3072], P('dp')
The draws below stay inside these ranges and needn't reach their ends.
Inputs may be any that keep to these rules, and one draw needn't show every extreme that they name: `doc_ids`: document numbers never fall along the sequence; every number from 0 to 3 occurs.
All inputs are finite; a program needn't handle non-finite values.
Results may differ from the reference program's by a relative error of at most 0.0052.
Values sent between devices are 32-bit elements; how exact they have to be, the bound alone decides.
A program may use at most 64 MiB of HBM per device.

```python
import math
import jax
import jax.numpy as jnp
import numpy as np
from jax import lax

H = 24
C = 128
DOCS = 4
SEQUENCE_LENGTH = 16384
NBLK = 128
F = 3072


def draw_log_decay(key, part):
    sequence_rows = jax.random.split(jax.random.fold_in(key, 71), 7)
    order = jax.random.permutation(sequence_rows[0], H)
    fast_count = H // 2
    fast_heads = order < fast_count
    slow_total = jnp.exp(jax.random.uniform(sequence_rows[1], (1, 1, H), jnp.float32, jnp.log(0.05), jnp.log(0.5)))
    slow_rate = slow_total / SEQUENCE_LENGTH
    fast_rate = jnp.exp(jax.random.uniform(sequence_rows[2], (1, 1, H), jnp.float32, jnp.log(1.0 / 50.0), jnp.log(1.0 / 30.0)))
    base_rate = jnp.where(fast_heads[None, None, :], fast_rate, slow_rate)
    block_count = SEQUENCE_LENGTH // C
    block_factor = jnp.exp(jax.random.uniform(sequence_rows[3], (1, block_count, 1, H), jnp.float32, jnp.log(0.5), jnp.log(2.0)))
    block_factor = jnp.broadcast_to(block_factor, (1, block_count, C, H)).reshape(1, SEQUENCE_LENGTH, H)
    roughness = jnp.exp(jax.random.uniform(sequence_rows[4], (1, SEQUENCE_LENGTH, H), jnp.float32, jnp.log(0.7), jnp.log(1.4)))
    reset_probability = base_rate * block_factor * roughness
    reset_positions = jax.random.randint(sequence_rows[5], (1, 3), 0, SEQUENCE_LENGTH)
    token_positions = jnp.arange(SEQUENCE_LENGTH)
    reset_hits = jnp.any(token_positions[None, :, None] == reset_positions[:, None, :], axis=2)
    keep_fraction = jax.random.uniform(sequence_rows[6], (1, SEQUENCE_LENGTH, 1), jnp.float32, 0.6, 0.8)
    reset_flags = jnp.where(reset_hits[:, :, None], jnp.log(keep_fraction), 0.0)
    return (reset_flags - reset_probability).astype(jnp.float32)[0]


def block_levels(own_key, shape, cuts, smallest, top_value):
    def one(position, shards_of):
        heights = jax.random.uniform(jax.random.fold_in(jax.random.fold_in(own_key, 6), position), (shards_of,), jnp.float32, smallest / len(cuts), top_value / len(cuts))
        return jnp.repeat(jnp.exp(heights), shape[position] // shards_of).reshape((-1,) + (1,) * (len(shape) - position - 1))

    factor_of = one(*cuts[0])
    for cut in cuts[1:]:
        factor_of = factor_of * one(*cut)
    return factor_of


def length_profile(amount, total, bound, lean):
    weights = [(1 << 20) // math.isqrt(standing ** lean) + 1 for standing in range(2, amount + 1)]
    rest, counts = total - bound - (amount - 1), [1] * (amount - 1)
    while rest > 0:
        candidates = [i for i in range(amount - 1) if counts[i] < bound]
        pool, left = sum([weights[i] for i in candidates]), rest
        for i in candidates:
            more = min(bound - counts[i], max(1, left * weights[i] // pool), rest)
            counts[i] = counts[i] + more
            rest = rest - more
    return np.array([bound] + counts)


def uneven_parts(stream_key, number_of, total, limit, lean):
    if number_of == 2:
        one = jax.random.randint(stream_key, (), max(1, total - limit), min(limit, total - 1) + 1)
        return jnp.stack([one, total - one])
    sizes = jnp.asarray(length_profile(number_of, total, limit, lean), jnp.int32)
    pairs = (number_of - 1) // 2
    giver, receiver = sizes[1:1 + 2 * pairs:2], sizes[2:2 + 2 * pairs:2]
    slack = jnp.minimum(giver - 1, limit - receiver)
    passed = jax.random.randint(jax.random.fold_in(stream_key, 1), (pairs,), 0, 1 << 20) % (slack + 1)
    sizes = sizes.at[1:1 + 2 * pairs:2].set(giver - passed).at[2:2 + 2 * pairs:2].set(receiver + passed)
    return sizes[jax.random.permutation(jax.random.fold_in(stream_key, 2), number_of)]


def normal_values(rng, extent, spread, reach, cuts=(), kind=jnp.bfloat16):
    values = spread * jax.random.normal(rng, extent, jnp.float32)
    if cuts:
        values = values * block_levels(rng, extent, cuts, -0.22, 0.18)
    return jnp.clip(values, -reach, reach).astype(kind)


def setup_inputs(seed: int = 0) -> dict:
    arg_keys = jax.random.split(jax.random.key(seed), 8)
    queries = normal_values(arg_keys[0], (SEQUENCE_LENGTH, F), 1.0, 6.0, ((0, 64), (1, 8)))
    keys = normal_values(arg_keys[1], (SEQUENCE_LENGTH, F), 1.0, 6.0, ((0, 64), (1, 8)))
    values = normal_values(arg_keys[2], (SEQUENCE_LENGTH, F), 1.0, 6.0, ((0, 64), (1, 8)))
    out_grad = normal_values(arg_keys[3], (SEQUENCE_LENGTH, F), 1.0, 6.0, ((0, 64), (1, 8)))
    log_decay = draw_log_decay(jax.random.fold_in(arg_keys[7], 71), 0)
    norm_gain = jnp.clip(1.0 + 0.18 * jax.random.normal(arg_keys[5], (F,), jnp.float32), 0.1, 1.9)
    doc_ids = jnp.searchsorted(jnp.cumsum(uneven_parts(arg_keys[6], DOCS, NBLK, NBLK // 2, 0)), jnp.arange(NBLK), side="right").astype(jnp.int32)
    return {"queries": queries, "keys": keys, "values": values, "out_grad": out_grad, "log_decay": log_decay, "norm_gain": norm_gain, "doc_ids": doc_ids}


EPSILON = 1e-06

def block_setup(log_block, length):
    cumulative = jnp.cumsum(log_block, axis=1)
    block_total = cumulative[:, -1, :]
    causal = (jnp.arange(length)[:, None] >= jnp.arange(length)[None, :]).astype(jnp.float32)
    log_gap = jnp.swapaxes(cumulative, 1, 2)
    decay_mask = jnp.exp(jnp.minimum(log_gap[..., :, None] - log_gap[..., None, :], 0.0)) * causal
    end_decay = jnp.exp(block_total[:, None, :] - cumulative)
    return (cumulative, block_total, decay_mask, end_decay)

def block_weights(query_blk, key_blk, decay_mask):
    scores = jnp.einsum('bthd,bshd->bhts', query_blk.astype(jnp.float32), key_blk.astype(jnp.float32))
    return (scores * decay_mask).astype(jnp.bfloat16)

def reference(queries, keys, values, out_grad, log_decay, norm_gain, doc_ids):
    queries = queries[None]
    keys = keys[None]
    values = values[None]
    out_grad = out_grad[None]
    log_decay = log_decay[None]
    doc_ids = doc_ids[None]
    batch, length, features = queries.shape
    head_count = log_decay.shape[2]
    head_width = features // head_count
    block_count = length // C

    def to_blocks(array):
        shaped = array.reshape((batch, block_count, C) + array.shape[2:])
        return jnp.swapaxes(shaped, 0, 1)

    def split_heads(array):
        return to_blocks(array.reshape(batch, length, head_count, head_width))
    query_all = split_heads(queries)
    key_all = split_heads(keys)
    value_all = split_heads(values)
    cot_all = split_heads(out_grad)
    decay_all = to_blocks(log_decay)
    previous = jnp.concatenate([jnp.full((batch, 1), -1, jnp.int32), doc_ids[:, :-1].astype(jnp.int32)], axis=1)
    carried_all = (previous == doc_ids.astype(jnp.int32)).astype(jnp.float32).T

    def forward_step(carry_pair, block_item):
        state, gain_acc = carry_pair
        query_blk, key_blk, value_blk, cot_blk, log_block, carried = block_item
        cumulative, block_total, decay_mask, end_decay = block_setup(log_block, query_blk.shape[1])
        weights = block_weights(query_blk, key_blk, decay_mask)
        local_out = jnp.einsum('bhts,bshd->bthd', weights.astype(jnp.float32), value_blk.astype(jnp.float32))
        query_scaled = query_blk.astype(jnp.float32) * (jnp.exp(cumulative) * carried[:, None, None])[..., None]
        far_out = jnp.einsum('bthd,bhde->bthe', query_scaled, state, precision=lax.Precision.HIGHEST)
        attention = (local_out + far_out).reshape(query_blk.shape[0], query_blk.shape[1], -1)
        inverse = lax.rsqrt(lax.optimization_barrier(jnp.mean(attention * attention, axis=2, keepdims=True)) + EPSILON)
        out_cot = cot_blk.astype(jnp.float32).reshape(attention.shape)
        weighted = out_cot * norm_gain
        inner = lax.optimization_barrier(jnp.mean(weighted * attention, axis=2, keepdims=True))
        attn_grad = ((weighted - attention * inner * inverse * inverse) * inverse).astype(jnp.bfloat16)
        gain_acc = gain_acc + lax.optimization_barrier(jnp.sum(out_cot * attention * inverse, axis=(0, 1)))
        key_scaled = (key_blk.astype(jnp.float32) * end_decay[..., None]).astype(jnp.bfloat16)
        update = jnp.einsum('bshd,bshe->bhde', key_scaled.astype(jnp.float32), value_blk.astype(jnp.float32))
        factor = carried[:, None] * jnp.exp(block_total)
        state = factor[..., None, None] * state + update
        return ((state, gain_acc), attn_grad.reshape(query_blk.shape))
    start_state = jnp.zeros((batch, head_count, head_width, head_width), jnp.float32)
    start_gain = jnp.zeros((features,), jnp.float32)
    (final_state, gain_grad), grad_all = lax.scan(forward_step, (start_state, start_gain), (query_all, key_all, value_all, cot_all, decay_all, carried_all))

    def backward_step(later_grad, block_item):
        query_blk, key_blk, value_blk, grad_blk, log_block, carried = block_item
        cumulative, block_total, decay_mask, end_decay = block_setup(log_block, query_blk.shape[1])
        weights = block_weights(query_blk, key_blk, decay_mask)
        value_local = jnp.einsum('bhts,bthd->bshd', weights.astype(jnp.float32), grad_blk.astype(jnp.float32))
        grad_dot = jnp.einsum('bthd,bshd->bhts', grad_blk.astype(jnp.float32), value_blk.astype(jnp.float32))
        grad_weights = (grad_dot * decay_mask).astype(jnp.bfloat16)
        key_local = jnp.einsum('bhts,bthd->bshd', grad_weights.astype(jnp.float32), query_blk.astype(jnp.float32))
        key_far = jnp.einsum('bshe,bhde->bshd', value_blk.astype(jnp.float32) * end_decay[..., None], later_grad, precision=lax.Precision.HIGHEST)
        value_far = jnp.einsum('bshd,bhde->bshe', key_blk.astype(jnp.float32) * end_decay[..., None], later_grad, precision=lax.Precision.HIGHEST)
        query_weighted = (query_blk.astype(jnp.float32) * jnp.exp(cumulative)[..., None]).astype(jnp.bfloat16)
        back_term = jnp.einsum('bthd,bthe->bhde', query_weighted.astype(jnp.float32), grad_blk.astype(jnp.float32))
        back_term = back_term * carried[:, None, None, None]
        factor = carried[:, None] * jnp.exp(block_total)
        later_grad = back_term + factor[..., None, None] * later_grad
        return (later_grad, ((key_local + key_far).astype(jnp.bfloat16), (value_local + value_far).astype(jnp.bfloat16)))
    final_grad, (key_blocks, value_blocks) = lax.scan(backward_step, start_state, (query_all, key_all, value_all, grad_all, decay_all, carried_all), reverse=True)

    def from_blocks(array):
        return jnp.swapaxes(array, 0, 1).reshape(batch, length, features)
    return (from_blocks(key_blocks)[0], from_blocks(value_blocks)[0], gain_grad)
```

```python
import jax
import jax.numpy as jnp
from jax import lax
from jax.experimental import pallas as pl
from jax.experimental.pallas import tpu as pltpu
from jax.sharding import PartitionSpec as P

C = 128
NZ = 16
EPSILON = 1e-06
MESH = pl.DeviceIdType.MESH
F32 = jnp.float32
BF16 = jnp.bfloat16


def dot(a, b, ca, cb, precision=None):
    return lax.dot_general(
        a, b, (((ca,), (cb,)), ((), ())), precision=precision, preferred_element_type=F32
    )


def split(x):
    high = x.astype(BF16)
    return high, (x - high.astype(F32)).astype(BF16)


def dot_split(high, low, b, cb):
    b_high, b_low = split(b)
    return dot(high, b_high, 1, cb) + (dot(high, b_low, 1, cb) + dot(low, b_high, 1, cb))


def kernel(
    heads,
    nx,
    ndp,
    q_hbm,
    k_hbm,
    v_hbm,
    o_hbm,
    log_hbm,
    gain_hbm,
    doc_hbm,
    kout_hbm,
    vout_hbm,
    gout_hbm,
    q_ref,
    k_ref,
    v_ref,
    o_ref,
    log_ref,
    gain_ref,
    doc_ref,
    kout,
    vout,
    gout,
    mask_ref,
    w_ref,
    u0_ref,
    qe_ref,
    qw_ref,
    ve_ref,
    ke_ref,
    part_ref,
    att_ref,
    ag_ref,
    bt1_ref,
    keyp_ref,
    valp_ref,
    info_s,
    info_r,
    u_s,
    u_r,
    pre_ref,
    x_s,
    x_r,
    a_s,
    a_r,
    st_s,
    st_r,
    b_s,
    b_r,
    bpre_ref,
    y_s,
    y_r,
    l_s,
    l_r,
    g_s,
    g_r,
    h_s,
    h_r,
    load_sem,
    store_sem,
    zs_sem,
    zr_sem,
    xs_sem,
    xr_sem,
    ds_sem,
    dr_sem,
):
    place = lax.axis_index("seq")
    me = lax.axis_index("dp")
    x = lax.div(place, NZ)
    z = lax.rem(place, NZ)
    rows = C // NZ
    tokens = 2 * C

    loads = [
        pltpu.make_async_copy(src, dst, load_sem.at[i])
        for i, (src, dst) in enumerate(
            (
                (log_hbm, log_ref),
                (doc_hbm, doc_ref),
                (k_hbm, k_ref),
                (v_hbm, v_ref),
                (q_hbm, q_ref),
                (o_hbm, o_ref),
                (gain_hbm, gain_ref),
            )
        )
    ]
    for load in loads:
        load.start()

    def each_z(run):
        def body(i, carry):
            half = lax.div(i + 1, 2)
            away = NZ // 2 + half * (1 - 2 * lax.rem(i, 2))
            run(lax.rem(z + away, NZ))
            return carry

        lax.fori_loop(0, NZ - 1, body, 0)

    def each_x(run):
        def body(i, carry):
            run(lax.rem(x + i, nx))
            return carry

        lax.fori_loop(1, nx, body, 0)

    def each_dp(run):
        def body(i, carry):
            run(lax.rem(me + i, ndp))
            return carry

        lax.fori_loop(1, ndp, body, 0)

    def z_copy(phase, src, dst, to, slot):
        return pltpu.make_async_remote_copy(
            src_ref=src,
            dst_ref=dst.at[slot],
            send_sem=zs_sem.at[phase, to],
            recv_sem=zr_sem.at[phase, slot],
            device_id={"seq": x * NZ + to},
            device_id_type=MESH,
        )

    def x_copy(phase, src, dst, to, slot):
        return pltpu.make_async_remote_copy(
            src_ref=src,
            dst_ref=dst.at[slot],
            send_sem=xs_sem.at[phase, to],
            recv_sem=xr_sem.at[phase, slot],
            device_id={"seq": to * NZ + z},
            device_id_type=MESH,
        )

    def d_copy(to, slot):
        return pltpu.make_async_remote_copy(
            src_ref=st_s,
            dst_ref=st_r.at[slot],
            send_sem=ds_sem.at[to],
            recv_sem=dr_sem.at[slot],
            device_id={"dp": to},
            device_id_type=MESH,
        )

    barrier = pltpu.get_barrier_semaphore()

    def greet(**where):
        pl.semaphore_signal(barrier, inc=1, device_id=where, device_id_type=MESH)

    each_z(lambda t: greet(seq=x * NZ + t))
    each_x(lambda t: greet(seq=t * NZ + z))
    each_dp(lambda t: greet(dp=t))

    for load in loads[:2]:
        load.wait()
    logs = jnp.concatenate(
        [log_ref[:, :C], log_ref[:, C:], jnp.zeros((8 - 2 * heads, C), F32)], axis=0
    )
    row_id = lax.broadcasted_iota(jnp.int32, (C, C), 0)
    col_id = lax.broadcasted_iota(jnp.int32, (C, C), 1)
    cum_rows = dot(logs, (row_id <= col_id).astype(F32), 1, 0, lax.Precision.HIGHEST)
    cum = cum_rows.T
    total = cum[C - 1 :, :]
    from_start = jnp.exp(cum)
    to_end = jnp.exp(total - cum)
    whole = jnp.exp(total)
    joined = jnp.where(doc_ref[0] == doc_ref[1], jnp.float32(1.0), jnp.float32(0.0))

    def at(table, block, head):
        r = block * heads + head
        return table[:, r : r + 1]

    def lanes(head):
        return slice(head * C, (head + 1) * C)

    for head in range(heads):
        info_s[:, lanes(head)] = jnp.broadcast_to(
            at(whole, 0, head) * (joined * at(whole, 1, head)), (1, C)
        )
    info_s[:, lanes(heads)] = jnp.full((1, C), doc_ref[0], jnp.int32).astype(F32)
    info_s[:, lanes(heads + 1)] = jnp.full((1, C), doc_ref[1], jnp.int32).astype(F32)

    for load in loads[2:4]:
        load.wait()
    for head in range(heads):
        updates = []
        for block in range(2):
            here = slice(block * C, (block + 1) * C)
            scaled = k_ref[here, lanes(head)].astype(F32) * at(to_end, block, head)
            updates.append(dot(scaled.astype(BF16), v_ref[here, lanes(head)], 0, 0))
        u0_ref[head] = updates[0]
        both = (joined * at(whole, 1, head)) * updates[0] + updates[1]
        u_s[:, head] = both.reshape(NZ, rows, C)

    pl.semaphore_wait(barrier, (NZ - 1) + (nx - 1) + (ndp - 1))
    each_z(lambda t: z_copy(0, info_s, info_r, t, z).start())
    each_z(lambda t: z_copy(1, u_s.at[t], u_r, t, z).start())
    info_r[z] = info_s[...]
    u_r[z] = u_s[z]

    for load in loads[4:]:
        load.wait()
    for head in range(heads):
        for block in range(2):
            here = slice(block * C, (block + 1) * C)
            r = block * heads + head
            gap = cum[:, r : r + 1] - cum_rows[r : r + 1, :]
            mask = jnp.where(row_id >= col_id, jnp.exp(jnp.minimum(gap, 0.0)), 0.0)
            mask_ref[r] = mask
            query = q_ref[here, lanes(head)]
            key = k_ref[here, lanes(head)]
            value = v_ref[here, lanes(head)]
            weights = (dot(query, key, 1, 1) * mask).astype(BF16)
            w_ref[r] = weights
            local = dot(weights, value, 1, 0)
            weighted = query.astype(F32) * at(from_start, block, head)
            qw_ref[r] = weighted.astype(BF16)
            if block == 1:
                high, low = split(weighted * joined)
                local = local + dot_split(high, low, u0_ref[head], 0)
                weighted = weighted * (joined * at(whole, 0, head))
            high, low = split(weighted)
            qe_ref[0, head, here] = high
            qe_ref[1, head, here] = low
            part_ref[here, lanes(head)] = local
            ending = at(to_end, block, head)
            if block == 0:
                ending = ending * (joined * at(whole, 1, head))
            high, low = split(value.astype(F32) * ending)
            ve_ref[0, head, here] = high
            ve_ref[1, head, here] = low
            high, low = split(key.astype(F32) * ending)
            ke_ref[0, head, here] = high
            ke_ref[1, head, here] = low

    each_z(lambda t: z_copy(0, info_s, info_r, t, t).wait_recv())

    def decay_of(t):
        return [
            jnp.broadcast_to(info_r[t, :, lanes(head)], (rows, C)) for head in range(heads)
        ]

    def first_doc(t):
        return info_r[t, :, lanes(heads)]

    def last_doc(t):
        return info_r[t, :, lanes(heads + 1)]

    def goes_on(later, earlier):
        return jnp.broadcast_to(jnp.where(later == earlier, 1.0, 0.0), (rows, C))

    each_z(lambda t: z_copy(1, u_s.at[t], u_r, t, t).wait_recv())
    state = [jnp.zeros((rows, C), F32)] * heads
    reach = [jnp.ones((rows, C), F32)] * heads
    for t in range(NZ):
        decay = decay_of(t)
        if t:
            keeps = goes_on(first_doc(t), last_doc(t - 1))
            state = [keeps * s for s in state]
            reach = [keeps * f for f in reach]
        for head in range(heads):
            pre_ref[0, t, head] = state[head]
            pre_ref[1, t, head] = reach[head]
        state = [decay[h] * state[h] + u_r[t, h] for h in range(heads)]
        reach = [decay[h] * reach[h] for h in range(heads)]
    for head in range(heads):
        x_s[head] = state[head]
        x_s[heads, head : head + 1] = reach[head][0:1]
    x_s[heads, heads : heads + 1] = first_doc(0)
    x_s[heads, heads + 1 : heads + 2] = last_doc(NZ - 1)
    each_x(lambda t: x_copy(0, x_s, x_r, t, x).start())
    x_r[x] = x_s[...]
    each_x(lambda t: x_copy(0, x_s, x_r, t, t).wait_recv())

    row_keeps = [None] + [
        goes_on(x_r[r, heads, heads : heads + 1], x_r[r - 1, heads, heads + 1 : heads + 2])
        for r in range(1, nx)
    ]
    row_reach = [
        [jnp.broadcast_to(x_r[r, heads, h : h + 1], (rows, C)) for h in range(heads)]
        for r in range(nx)
    ]
    entering = [jnp.zeros((rows, C), F32)] * heads
    chosen = entering
    for r in range(1, nx):
        entering = [
            row_keeps[r] * (x_r[r - 1, h] + row_reach[r - 1][h] * entering[h])
            for h in range(heads)
        ]
        chosen = [jnp.where(x == r, entering[h], chosen[h]) for h in range(heads)]
    for t in range(NZ):
        for head in range(heads):
            a_s[t, head] = pre_ref[0, t, head] + pre_ref[1, t, head] * chosen[head]
    each_z(lambda t: z_copy(2, a_s.at[t], a_r, t, z).start())
    a_r[z] = a_s[z]
    each_z(lambda t: z_copy(2, a_s.at[t], a_r, t, t).wait_recv())

    squares = jnp.zeros((tokens, C), F32)
    inners = jnp.zeros((tokens, C), F32)
    for head in range(heads):
        came = a_r[:, head].reshape(C, C)
        attention = part_ref[:, lanes(head)] + dot_split(qe_ref[0, head], qe_ref[1, head], came, 0)
        att_ref[:, lanes(head)] = attention
        wanted = o_ref[:, lanes(head)].astype(F32) * gain_ref[:, lanes(head)]
        squares = squares + attention * attention
        inners = inners + wanted * attention
    lane = lax.broadcasted_iota(jnp.int32, (tokens, C), 1)
    stats = jnp.where(
        lane == 0,
        jnp.sum(squares, axis=1, keepdims=True),
        jnp.sum(inners, axis=1, keepdims=True),
    ).T
    st_s[...] = stats[0:2]
    each_dp(lambda t: d_copy(t, me).start())
    st_r[me] = st_s[...]
    each_dp(lambda t: d_copy(t, t).wait_recv())
    sums = st_r[0]
    for r in range(1, ndp):
        sums = sums + st_r[r]
    means = sums / (ndp * heads * C)
    inverse = lax.rsqrt(means[0:1] + EPSILON)
    bend = means[1:2] * inverse * inverse
    side = lax.broadcasted_iota(jnp.int32, (8, tokens), 0)
    columns = jnp.where(side == 0, inverse, bend).T
    inverse = columns[:, 0:1]
    bend = columns[:, 1:2]

    for head in range(heads):
        attention = att_ref[:, lanes(head)]
        out_cot = o_ref[:, lanes(head)].astype(F32)
        wanted = out_cot * gain_ref[:, lanes(head)]
        grad = ((wanted - attention * bend) * inverse).astype(BF16)
        ag_ref[:, lanes(head)] = grad
        back = [
            dot(qw_ref[b * heads + head], grad[b * C : (b + 1) * C], 0, 0) for b in range(2)
        ]
        back_next = joined * back[1]
        bt1_ref[head] = back_next
        b_s[:, head] = (back[0] + at(whole, 0, head) * back_next).reshape(NZ, rows, C)
    each_z(lambda t: z_copy(3, b_s.at[t], b_r, t, z).start())
    b_r[z] = b_s[z]

    for head in range(heads):
        attention = att_ref[:, lanes(head)]
        out_cot = o_ref[:, lanes(head)].astype(F32)
        g_s[:, lanes(head)] = jnp.sum(out_cot * attention * inverse, axis=0, keepdims=True)
    each_z(lambda t: z_copy(4, g_s, g_r, t, z).start())
    g_r[z] = g_s[...]

    for head in range(heads):
        for block in range(2):
            here = slice(block * C, (block + 1) * C)
            r = block * heads + head
            grad = ag_ref[here, lanes(head)]
            value = v_ref[here, lanes(head)]
            key = k_ref[here, lanes(head)]
            value_part = dot(w_ref[r], grad, 0, 0)
            grad_weights = (dot(grad, value, 1, 1) * mask_ref[r]).astype(BF16)
            key_part = dot(grad_weights, q_ref[here, lanes(head)], 0, 0)
            if block == 0:
                ending = at(to_end, 0, head)
                high, low = split(value.astype(F32) * ending)
                key_part = key_part + dot_split(high, low, bt1_ref[head], 1)
                high, low = split(key.astype(F32) * ending)
                value_part = value_part + dot_split(high, low, bt1_ref[head], 0)
            keyp_ref[here, lanes(head)] = key_part
            valp_ref[here, lanes(head)] = value_part

    each_z(lambda t: z_copy(3, b_s.at[t], b_r, t, t).wait_recv())
    state = [jnp.zeros((rows, C), F32)] * heads
    reach = [jnp.ones((rows, C), F32)] * heads
    for t in range(NZ - 1, -1, -1):
        decay = decay_of(t)
        for head in range(heads):
            bpre_ref[0, t, head] = state[head]
            bpre_ref[1, t, head] = reach[head]
        state = [decay[h] * state[h] + b_r[t, h] for h in range(heads)]
        reach = [decay[h] * reach[h] for h in range(heads)]
        if t:
            keeps = goes_on(first_doc(t), last_doc(t - 1))
            state = [keeps * s for s in state]
            reach = [keeps * f for f in reach]
    for head in range(heads):
        y_s[head] = state[head]
    each_x(lambda t: x_copy(1, y_s, y_r, t, x).start())
    y_r[x] = y_s[...]

    each_z(lambda t: z_copy(4, g_s, g_r, t, t).wait_recv())
    row_gain = g_r[0]
    for t in range(1, NZ):
        row_gain = row_gain + g_r[t]
    h_s[...] = row_gain
    each_x(lambda t: x_copy(2, h_s, h_r, t, x).start())
    h_r[x] = h_s[...]

    each_x(lambda t: x_copy(1, y_s, y_r, t, t).wait_recv())
    entering = [jnp.zeros((rows, C), F32)] * heads
    chosen = entering
    for r in range(nx - 2, -1, -1):
        entering = [
            row_keeps[r + 1] * (y_r[r + 1, h] + row_reach[r + 1][h] * entering[h])
            for h in range(heads)
        ]
        chosen = [jnp.where(x == r, entering[h], chosen[h]) for h in range(heads)]
    for t in range(NZ):
        for head in range(heads):
            l_s[t, head] = bpre_ref[0, t, head] + bpre_ref[1, t, head] * chosen[head]
    each_z(lambda t: z_copy(5, l_s.at[t], l_r, t, z).start())
    l_r[z] = l_s[z]

    each_x(lambda t: x_copy(2, h_s, h_r, t, t).wait_recv())
    gain = h_r[0]
    for r in range(1, nx):
        gain = gain + h_r[r]
    gout[...] = gain
    stores = [
        pltpu.make_async_copy(src, dst, store_sem.at[i])
        for i, (src, dst) in enumerate(((kout, kout_hbm), (vout, vout_hbm), (gout, gout_hbm)))
    ]
    stores[2].start()

    each_z(lambda t: z_copy(5, l_s.at[t], l_r, t, t).wait_recv())
    for head in range(heads):
        came = l_r[:, head].reshape(C, C)
        far = dot_split(ve_ref[0, head], ve_ref[1, head], came, 1)
        kout[:, lanes(head)] = (keyp_ref[:, lanes(head)] + far).astype(BF16)
        far = dot_split(ke_ref[0, head], ke_ref[1, head], came, 0)
        vout[:, lanes(head)] = (valp_ref[:, lanes(head)] + far).astype(BF16)
    stores[0].start()
    stores[1].start()

    each_z(lambda t: z_copy(0, info_s, info_r, t, t).wait_send())
    each_z(lambda t: z_copy(1, u_s.at[t], u_r, t, t).wait_send())
    each_z(lambda t: z_copy(2, a_s.at[t], a_r, t, t).wait_send())
    each_z(lambda t: z_copy(3, b_s.at[t], b_r, t, t).wait_send())
    each_z(lambda t: z_copy(4, g_s, g_r, t, t).wait_send())
    each_z(lambda t: z_copy(5, l_s.at[t], l_r, t, t).wait_send())
    each_x(lambda t: x_copy(0, x_s, x_r, t, t).wait_send())
    each_x(lambda t: x_copy(1, y_s, y_r, t, t).wait_send())
    each_x(lambda t: x_copy(2, h_s, h_r, t, t).wait_send())
    each_dp(lambda t: d_copy(t, t).wait_send())
    for store in stores:
        store.wait()


def per_device(queries, keys, values, out_grad, log_decay, norm_gain, doc_ids):
    tokens, features = queries.shape
    heads = log_decay.shape[1]
    ndp = lax.axis_size("dp")
    nx = lax.axis_size("seq") // NZ
    rows = C // NZ
    wide = (tokens, features)
    squares = (2 * heads, C, C)
    table = (NZ, heads, rows, C)
    anywhere = pl.BlockSpec(memory_space=pl.ANY)
    scratch = [
        pltpu.VMEM(wide, BF16),
        pltpu.VMEM(wide, BF16),
        pltpu.VMEM(wide, BF16),
        pltpu.VMEM(wide, BF16),
        pltpu.VMEM((heads, tokens), F32),
        pltpu.VMEM((1, features), F32),
        pltpu.SMEM((2,), jnp.int32),
        pltpu.VMEM(wide, BF16),
        pltpu.VMEM(wide, BF16),
        pltpu.VMEM((1, features), F32),
        pltpu.VMEM(squares, F32),
        pltpu.VMEM(squares, BF16),
        pltpu.VMEM((heads, C, C), F32),
        pltpu.VMEM((2, heads, tokens, C), BF16),
        pltpu.VMEM(squares, BF16),
        pltpu.VMEM((2, heads, tokens, C), BF16),
        pltpu.VMEM((2, heads, tokens, C), BF16),
        pltpu.VMEM(wide, F32),
        pltpu.VMEM(wide, F32),
        pltpu.VMEM(wide, BF16),
        pltpu.VMEM((heads, C, C), F32),
        pltpu.VMEM(wide, F32),
        pltpu.VMEM(wide, F32),
        pltpu.VMEM((1, (heads + 2) * C), F32),
        pltpu.VMEM((NZ, 1, (heads + 2) * C), F32),
        pltpu.VMEM(table, F32),
        pltpu.VMEM(table, F32),
        pltpu.VMEM((2,) + table, F32),
        pltpu.VMEM((heads + 1, rows, C), F32),
        pltpu.VMEM((nx, heads + 1, rows, C), F32),
        pltpu.VMEM(table, F32),
        pltpu.VMEM(table, F32),
        pltpu.VMEM((2, tokens), F32),
        pltpu.VMEM((ndp, 2, tokens), F32),
        pltpu.VMEM(table, F32),
        pltpu.VMEM(table, F32),
        pltpu.VMEM((2,) + table, F32),
        pltpu.VMEM((heads, rows, C), F32),
        pltpu.VMEM((nx, heads, rows, C), F32),
        pltpu.VMEM(table, F32),
        pltpu.VMEM(table, F32),
        pltpu.VMEM((1, features), F32),
        pltpu.VMEM((NZ, 1, features), F32),
        pltpu.VMEM((1, features), F32),
        pltpu.VMEM((nx, 1, features), F32),
        pltpu.SemaphoreType.DMA((7,)),
        pltpu.SemaphoreType.DMA((3,)),
        pltpu.SemaphoreType.DMA((6, NZ)),
        pltpu.SemaphoreType.DMA((6, NZ)),
        pltpu.SemaphoreType.DMA((3, nx)),
        pltpu.SemaphoreType.DMA((3, nx)),
        pltpu.SemaphoreType.DMA((ndp,)),
        pltpu.SemaphoreType.DMA((ndp,)),
    ]

    def body(*refs):
        kernel(heads, nx, ndp, *refs)

    key_grad, value_grad, gain_grad = pl.pallas_call(
        body,
        out_shape=(
            jax.ShapeDtypeStruct(wide, BF16),
            jax.ShapeDtypeStruct(wide, BF16),
            jax.ShapeDtypeStruct((1, features), F32),
        ),
        in_specs=[anywhere] * 7,
        out_specs=(anywhere, anywhere, anywhere),
        scratch_shapes=scratch,
        compiler_params=pltpu.CompilerParams(collective_id=0, has_side_effects=True),
        name="attention_core",
    )(
        queries,
        keys,
        values,
        out_grad,
        log_decay.T,
        norm_gain.reshape(1, features),
        doc_ids,
    )
    return key_grad, value_grad, gain_grad.reshape(features)


def solution(mesh):
    placed = (
        P("seq", "dp"),
        P("seq", "dp"),
        P("seq", "dp"),
        P("seq", "dp"),
        P("seq", "dp"),
        P("dp"),
        P("seq"),
    )
    return jax.shard_map(
        per_device,
        mesh=mesh,
        in_specs=placed,
        out_specs=(P("seq", "dp"), P("seq", "dp"), P("dp")),
        check_vma=False,
    )
```

```python
from typing import Any, NamedTuple

import jax
import jax.numpy as jnp
from jax import lax
from jax.experimental import pallas as pl
from jax.experimental.pallas import tpu as pltpu
from jax.sharding import PartitionSpec as P

C = 128
NZ = 16
EPSILON = 1e-06
MESH = pl.DeviceIdType.MESH
F32 = jnp.float32
BF16 = jnp.bfloat16


def dot(a, b, ca, cb, precision=None):
    return lax.dot_general(
        a, b, (((ca,), (cb,)), ((), ())), precision=precision, preferred_element_type=F32
    )


def split(x):
    high = x.astype(BF16)
    return high, (x - high.astype(F32)).astype(BF16)


def dot_split(high, low, b, cb):
    b_high, b_low = split(b)
    return dot(high, b_high, 1, cb) + (dot(high, b_low, 1, cb) + dot(low, b_high, 1, cb))


class Scan(NamedTuple):
    up_s: Any
    up_r: Any
    pre: Any
    x_s: Any
    x_r: Any
    down_s: Any
    down_r: Any


def groups_of(heads):
    return ((0,), tuple(range(1, heads)))


def kernel(heads, nx, ndp, ins, outs, local, info, scans, norm, gains, sems):
    q_hbm, k_hbm, v_hbm, o_hbm, log_hbm, gain_hbm, doc_hbm = ins
    kout, vout, gout = outs
    (
        (q_ref, k_ref, v_ref, o_ref, log_ref, gain_ref, doc_ref),
        (mask_ref, w_ref, u0_ref, qe_ref, qw_ref, ve_ref, ke_ref),
        (part_ref, att_ref, ag_ref, bt1_ref, keyp_ref, valp_ref),
    ) = local
    info_s, info_r, keep_ref, step_ref, reach_ref, end_ref, row_s, row_r = info
    st_s, st_r = norm
    g_s, g_r, h_s, h_r = gains
    load_sem, zs_sem, zr_sem, xs_sem, xr_sem, ds_sem, dr_sem = sems
    groups = groups_of(heads)
    place = lax.axis_index("seq")
    me = lax.axis_index("dp")
    x = lax.div(place, NZ)
    z = lax.rem(place, NZ)
    rows = C // NZ
    tokens = 2 * C

    loads = [
        pltpu.make_async_copy(src, dst, load_sem.at[i])
        for i, (src, dst) in enumerate(
            (
                (log_hbm, log_ref),
                (doc_hbm, doc_ref),
                (k_hbm, k_ref),
                (v_hbm, v_ref),
                (q_hbm, q_ref),
                (o_hbm, o_ref),
                (gain_hbm, gain_ref.at[0]),
            )
        )
    ]
    for load in loads:
        load.start()

    def each_z(run):
        def body(i, carry):
            half = lax.div(i + 1, 2)
            away = NZ // 2 + half * (1 - 2 * lax.rem(i, 2))
            run(lax.rem(z + away, NZ))
            return carry

        lax.fori_loop(0, NZ - 1, body, 0)

    def each_x(run):
        def body(i, carry):
            run(lax.rem(x + i, nx))
            return carry

        lax.fori_loop(1, nx, body, 0)

    def each_dp(run):
        def body(i, carry):
            run(lax.rem(me + i, ndp))
            return carry

        lax.fori_loop(1, ndp, body, 0)

    sent = []

    def exchange(each, where, mine, count, source, slots, send_sem, recv_sem):
        def start(t):
            pltpu.make_async_remote_copy(
                src_ref=source(t),
                dst_ref=slots.at[mine],
                send_sem=send_sem,
                recv_sem=recv_sem,
                device_id=where(t),
                device_id_type=MESH,
            ).start()

        each(start)
        slots[mine] = source(mine)[...]
        others = slots.at[pl.ds(0, count - 1)]
        whole = pltpu.make_async_remote_copy(
            src_ref=others,
            dst_ref=others,
            send_sem=send_sem,
            recv_sem=recv_sem,
            device_id=where(mine),
            device_id_type=MESH,
        )
        sent.append(whole)
        return whole.wait_recv

    def over_z(phase, source, slots):
        return exchange(
            each_z,
            lambda t: {"seq": x * NZ + t},
            z,
            NZ,
            source,
            slots,
            zs_sem.at[phase],
            zr_sem.at[phase],
        )

    def over_x(phase, source, slots):
        return exchange(
            each_x,
            lambda t: {"seq": t * NZ + z},
            x,
            nx,
            lambda t: source,
            slots,
            xs_sem.at[phase],
            xr_sem.at[phase],
        )

    barrier = pltpu.get_barrier_semaphore()

    def greet(**where):
        pl.semaphore_signal(barrier, inc=1, device_id=where, device_id_type=MESH)

    each_z(lambda t: greet(seq=x * NZ + t))
    each_x(lambda t: greet(seq=t * NZ + z))
    each_dp(lambda t: greet(dp=t))

    for load in loads[:2]:
        load.wait()
    logs = jnp.concatenate(
        [log_ref[:, :C], log_ref[:, C:], jnp.zeros((8 - 2 * heads, C), F32)], axis=0
    )
    row_id = lax.broadcasted_iota(jnp.int32, (C, C), 0)
    col_id = lax.broadcasted_iota(jnp.int32, (C, C), 1)
    cum_rows = dot(logs, (row_id <= col_id).astype(F32), 1, 0, lax.Precision.HIGHEST)
    cum = cum_rows.T
    total = cum[C - 1 :, :]
    from_start = jnp.exp(cum)
    to_end = jnp.exp(total - cum)
    whole = jnp.exp(total)
    joined = jnp.where(doc_ref[0] == doc_ref[1], jnp.float32(1.0), jnp.float32(0.0))

    def at(table, block, head):
        r = block * heads + head
        return table[:, r : r + 1]

    def lanes(head):
        return slice(head * C, (head + 1) * C)

    lane = lax.broadcasted_iota(jnp.int32, (1, C), 1)
    line = jnp.zeros((1, C), F32)
    for head in range(heads):
        line = jnp.where(
            lane == head, at(whole, 0, head) * (joined * at(whole, 1, head)), line
        )
    for i in range(2):
        document = jnp.full((1, C), doc_ref[i], jnp.int32).astype(F32)
        line = jnp.where(lane == heads + i, document, line)
    info_s[...] = line

    for load in loads[2:4]:
        load.wait()
    for group, scan in zip(groups, scans[0]):
        for i, head in enumerate(group):
            updates = []
            for block in range(2):
                here = slice(block * C, (block + 1) * C)
                scaled = k_ref[here, lanes(head)].astype(F32) * at(to_end, block, head)
                updates.append(dot(scaled.astype(BF16), v_ref[here, lanes(head)], 0, 0))
            u0_ref[head] = updates[0]
            both = (joined * at(whole, 1, head)) * updates[0] + updates[1]
            scan.up_s[:, i] = both.reshape(NZ, rows, C)

    pl.semaphore_wait(barrier, (NZ - 1) + (nx - 1) + (ndp - 1))
    info_wait = over_z(0, lambda t: info_s, info_r)
    up_waits = [
        over_z(1 + g, lambda t, scan=scan: scan.up_s.at[t], scan.up_r)
        for g, scan in enumerate(scans[0])
    ]

    info_wait()

    def tile(line, i):
        return jnp.broadcast_to(line[:, i : i + 1], (rows, C))

    def goes_on(later, earlier):
        return jnp.where(
            later[:, heads : heads + 1] == earlier[:, heads + 1 : heads + 2], 1.0, 0.0
        )

    line = info_r[0]
    reach = jnp.ones((1, C), F32)
    for t in range(NZ):
        if t:
            earlier, line = line, info_r[t]
            keeps = goes_on(line, earlier)
            keep_ref[t] = jnp.broadcast_to(keeps, (rows, C))
            for head in range(heads):
                step_ref[0, t, head] = tile(keeps * earlier, head)
                step_ref[1, t, head] = tile(keeps * line, head)
            reach = reach * (keeps * earlier)
        for head in range(heads):
            reach_ref[0, t, head] = tile(reach, head)
    first, last = info_r[0], info_r[NZ - 1]
    row_s[...] = jnp.where(
        lane < heads, reach * last, jnp.where(lane == heads, first, last)
    )
    row_wait = over_x(0, row_s, row_r)
    for head in range(heads):
        end_ref[0, head] = tile(last, head)
        end_ref[1, head] = tile(first, head)
    reach = jnp.ones((1, C), F32)
    for t in range(NZ - 1, -1, -1):
        for head in range(heads):
            reach_ref[1, t, head] = tile(reach, head)
        if t:
            reach = reach * (goes_on(info_r[t], info_r[t - 1]) * info_r[t])

    for load in loads[4:]:
        load.wait()
    for head in range(heads):
        for block in range(2):
            here = slice(block * C, (block + 1) * C)
            r = block * heads + head
            gap = cum[:, r : r + 1] - cum_rows[r : r + 1, :]
            mask = jnp.where(row_id >= col_id, jnp.exp(jnp.minimum(gap, 0.0)), 0.0)
            mask_ref[r] = mask
            query = q_ref[here, lanes(head)]
            key = k_ref[here, lanes(head)]
            value = v_ref[here, lanes(head)]
            weights = (dot(query, key, 1, 1) * mask).astype(BF16)
            w_ref[r] = weights
            near = dot(weights, value, 1, 0)
            weighted = query.astype(F32) * at(from_start, block, head)
            qw_ref[r] = weighted.astype(BF16)
            if block == 1:
                high, low = split(weighted * joined)
                near = near + dot_split(high, low, u0_ref[head], 0)
                weighted = weighted * (joined * at(whole, 0, head))
            high, low = split(weighted)
            qe_ref[0, head, here] = high
            qe_ref[1, head, here] = low
            part_ref[here, lanes(head)] = near
            ending = at(to_end, block, head)
            if block == 0:
                ending = ending * (joined * at(whole, 1, head))
            high, low = split(value.astype(F32) * ending)
            ve_ref[0, head, here] = high
            ve_ref[1, head, here] = low
            high, low = split(key.astype(F32) * ending)
            ke_ref[0, head, here] = high
            ke_ref[1, head, here] = low
    row_wait()
    row_lines = [row_r[r] for r in range(nx)]

    def scan_row(back, scan, group):
        count = len(group)
        state = [jnp.zeros((rows, C), F32)] * count
        order = range(NZ - 1, -1, -1) if back else range(NZ)
        for t in order:
            for i in range(count):
                scan.pre[t, i] = state[i]
            if t != order[-1]:
                link = t if back else t + 1
                state = [
                    step_ref[back, link, head] * state[i] + keep_ref[link] * scan.up_r[t, i]
                    for i, head in enumerate(group)
                ]
            else:
                for i, head in enumerate(group):
                    scan.x_s[i] = end_ref[back, head] * state[i] + scan.up_r[t, i]

    def scan_rows(back, scan, group):
        count = len(group)
        entering = [jnp.zeros((rows, C), F32)] * count
        chosen = entering
        for r in range(nx - 2, -1, -1) if back else range(1, nx):
            other = r + 1 if back else r - 1
            keeps = goes_on(row_lines[max(r, other)], row_lines[min(r, other)])
            entering = [
                jnp.broadcast_to(keeps, (rows, C)) * scan.x_r[other, i]
                + tile(keeps * row_lines[other], head) * entering[i]
                for i, head in enumerate(group)
            ]
            chosen = [jnp.where(x == r, entering[i], chosen[i]) for i in range(count)]
        for t in range(NZ):
            for i, head in enumerate(group):
                scan.down_s[t, i] = scan.pre[t, i] + reach_ref[back, t, head] * chosen[i]

    def scan_all(back, up_waits):
        base = 1 + back * 2 * len(groups)
        x_waits, down_waits = [], []
        for g, (group, scan) in enumerate(zip(groups, scans[back])):
            up_waits[g]()
            scan_row(back, scan, group)
            x_waits.append(over_x(1 + back * len(groups) + g, scan.x_s, scan.x_r))
        for g, (group, scan) in enumerate(zip(groups, scans[back])):
            x_waits[g]()
            scan_rows(back, scan, group)
            down_waits.append(
                over_z(
                    base + len(groups) + g, lambda t, scan=scan: scan.down_s.at[t], scan.down_r
                )
            )
        return down_waits

    down_waits = scan_all(0, up_waits)

    squares = jnp.zeros((tokens, C), F32)
    inners = jnp.zeros((tokens, C), F32)
    for group, scan, arrived in zip(groups, scans[0], down_waits):
        arrived()
        for i, head in enumerate(group):
            came = scan.down_r[:, i].reshape(C, C)
            far = dot_split(qe_ref[0, head], qe_ref[1, head], came, 0)
            attention = part_ref[:, lanes(head)] + far
            att_ref[:, lanes(head)] = attention
            wanted = o_ref[:, lanes(head)].astype(F32) * gain_ref[:, lanes(head)]
            squares = squares + attention * attention
            inners = inners + wanted * attention
    lane = lax.broadcasted_iota(jnp.int32, (tokens, C), 1)
    stats = jnp.where(
        lane == 0,
        jnp.sum(squares, axis=1, keepdims=True),
        jnp.sum(inners, axis=1, keepdims=True),
    ).T
    st_s[...] = stats[0:2]
    exchange(each_dp, lambda t: {"dp": t}, me, ndp, lambda t: st_s, st_r, ds_sem, dr_sem)()
    sums = st_r[0]
    for r in range(1, ndp):
        sums = sums + st_r[r]
    means = sums / (ndp * heads * C)
    inverse = lax.rsqrt(means[0:1] + EPSILON)
    bend = means[1:2] * inverse * inverse
    side = lax.broadcasted_iota(jnp.int32, (8, tokens), 0)
    columns = jnp.where(side == 0, inverse, bend).T
    inverse = columns[:, 0:1]
    bend = columns[:, 1:2]

    up_waits = []
    for g, (group, scan) in enumerate(zip(groups, scans[1])):
        for i, head in enumerate(group):
            attention = att_ref[:, lanes(head)]
            wanted = o_ref[:, lanes(head)].astype(F32) * gain_ref[:, lanes(head)]
            grad = ((wanted - attention * bend) * inverse).astype(BF16)
            ag_ref[:, lanes(head)] = grad
            back = [
                dot(qw_ref[b * heads + head], grad[b * C : (b + 1) * C], 0, 0) for b in range(2)
            ]
            back_next = joined * back[1]
            bt1_ref[head] = back_next
            both = back[0] + at(whole, 0, head) * back_next
            scan.up_s[:, i] = both.reshape(NZ, rows, C)
        up_waits.append(
            over_z(
                1 + 2 * len(groups) + g, lambda t, scan=scan: scan.up_s.at[t], scan.up_r
            )
        )

    for head in range(heads):
        attention = att_ref[:, lanes(head)]
        out_cot = o_ref[:, lanes(head)].astype(F32)
        g_s[:, lanes(head)] = jnp.sum(out_cot * attention * inverse, axis=0, keepdims=True)
    gain_wait = over_z(1 + 4 * len(groups), lambda t: g_s, g_r)

    for head in range(heads):
        for block in range(2):
            here = slice(block * C, (block + 1) * C)
            r = block * heads + head
            grad = ag_ref[here, lanes(head)]
            value = v_ref[here, lanes(head)]
            key = k_ref[here, lanes(head)]
            value_part = dot(w_ref[r], grad, 0, 0)
            grad_weights = (dot(grad, value, 1, 1) * mask_ref[r]).astype(BF16)
            key_part = dot(grad_weights, q_ref[here, lanes(head)], 0, 0)
            if block == 0:
                ending = at(to_end, 0, head)
                high, low = split(value.astype(F32) * ending)
                key_part = key_part + dot_split(high, low, bt1_ref[head], 1)
                high, low = split(key.astype(F32) * ending)
                value_part = value_part + dot_split(high, low, bt1_ref[head], 0)
            keyp_ref[here, lanes(head)] = key_part
            valp_ref[here, lanes(head)] = value_part

    down_waits = scan_all(1, up_waits)

    gain_wait()
    row_gain = g_r[0]
    for t in range(1, NZ):
        row_gain = row_gain + g_r[t]
    h_s[...] = row_gain
    over_x(1 + 2 * len(groups), h_s, h_r)()
    gain = h_r[0]
    for r in range(1, nx):
        gain = gain + h_r[r]
    gout[...] = gain.reshape(heads * C)

    for group, scan, arrived in zip(groups, scans[1], down_waits):
        arrived()
        for i, head in enumerate(group):
            came = scan.down_r[:, i].reshape(C, C)
            far = dot_split(ve_ref[0, head], ve_ref[1, head], came, 1)
            kout[:, lanes(head)] = (keyp_ref[:, lanes(head)] + far).astype(BF16)
            far = dot_split(ke_ref[0, head], ke_ref[1, head], came, 0)
            vout[:, lanes(head)] = (valp_ref[:, lanes(head)] + far).astype(BF16)

    for copies in sent:
        copies.wait_send()


def per_device(queries, keys, values, out_grad, log_decay, norm_gain, doc_ids):
    tokens, features = queries.shape
    heads = log_decay.shape[1]
    ndp = lax.axis_size("dp")
    nx = lax.axis_size("seq") // NZ
    rows = C // NZ
    groups = groups_of(heads)
    wide = (tokens, features)
    squares = (2 * heads, C, C)
    halves = (2, heads, tokens, C)
    anywhere = pl.BlockSpec(memory_space=pl.ANY)
    vmem = pltpu.VMEM
    dma = pltpu.SemaphoreType.DMA
    local = (
        (
            vmem(wide, BF16),
            vmem(wide, BF16),
            vmem(wide, BF16),
            vmem(wide, BF16),
            vmem((heads, tokens), F32),
            vmem((1, features), F32),
            pltpu.SMEM((2,), jnp.int32),
        ),
        (
            vmem(squares, F32),
            vmem(squares, BF16),
            vmem((heads, C, C), F32),
            vmem(halves, BF16),
            vmem(squares, BF16),
            vmem(halves, BF16),
            vmem(halves, BF16),
        ),
        (
            vmem(wide, F32),
            vmem(wide, F32),
            vmem(wide, BF16),
            vmem((heads, C, C), F32),
            vmem(wide, F32),
            vmem(wide, F32),
        ),
    )
    info = (
        vmem((1, C), F32),
        vmem((NZ, 1, C), F32),
        vmem((NZ, rows, C), F32),
        vmem((2, NZ, heads, rows, C), F32),
        vmem((2, NZ, heads, rows, C), F32),
        vmem((2, heads, rows, C), F32),
        vmem((1, C), F32),
        vmem((nx, 1, C), F32),
    )

    def scan_of(count):
        table = (NZ, count, rows, C)
        return Scan(
            up_s=vmem(table, F32),
            up_r=vmem(table, F32),
            pre=vmem(table, F32),
            x_s=vmem((count, rows, C), F32),
            x_r=vmem((nx, count, rows, C), F32),
            down_s=vmem(table, F32),
            down_r=vmem(table, F32),
        )

    scans = tuple(tuple(scan_of(len(group)) for group in groups) for _ in range(2))
    norm = (vmem((2, tokens), F32), vmem((ndp, 2, tokens), F32))
    gains = (
        vmem((1, features), F32),
        vmem((NZ, 1, features), F32),
        vmem((1, features), F32),
        vmem((nx, 1, features), F32),
    )
    z_count, x_count = 2 + 4 * len(groups), 2 + 2 * len(groups)
    sems = (
        dma((7,)),
        dma((z_count,)),
        dma((z_count,)),
        dma((x_count,)),
        dma((x_count,)),
        dma,
        dma,
    )
    scratch, tree = jax.tree.flatten((local, info, scans, norm, gains, sems))

    def body(*refs):
        kernel(heads, nx, ndp, refs[:7], refs[7:10], *jax.tree.unflatten(tree, refs[10:]))

    return pl.pallas_call(
        body,
        out_shape=(vmem(wide, BF16), vmem(wide, BF16), vmem((features,), F32)),
        in_specs=[anywhere] * 7,
        out_specs=(pl.BlockSpec(memory_space=pltpu.VMEM),) * 3,
        scratch_shapes=scratch,
        compiler_params=pltpu.CompilerParams(collective_id=0, has_side_effects=True),
        name="attention_core",
    )(queries, keys, values, out_grad, log_decay.T, norm_gain, doc_ids)


def solution(mesh):
    placed = (
        P("seq", "dp"),
        P("seq", "dp"),
        P("seq", "dp"),
        P("seq", "dp"),
        P("seq", "dp"),
        P("dp"),
        P("seq"),
    )
    return jax.shard_map(
        per_device,
        mesh=mesh,
        in_specs=placed,
        out_specs=(P("seq", "dp"), P("seq", "dp"), P("dp")),
        check_vma=False,
    )
```

```python
from typing import Any, NamedTuple

import jax
import jax.numpy as jnp
from jax import lax
from jax.experimental import pallas as pl
from jax.experimental.pallas import tpu as pltpu
from jax.sharding import PartitionSpec as P

C = 128
NZ = 16
EPSILON = 1e-06
MESH = pl.DeviceIdType.MESH
F32 = jnp.float32
BF16 = jnp.bfloat16


def dot(a, b, ca, cb, precision=None):
    return lax.dot_general(
        a, b, (((ca,), (cb,)), ((), ())), precision=precision, preferred_element_type=F32
    )


def split(x):
    high = x.astype(BF16)
    return high, (x - high.astype(F32)).astype(BF16)


def dot_split(a, b, cb):
    high, low = split(b)
    both = dot(a, jnp.concatenate([high, low], axis=1 - cb), 1, cb)
    return both[:, :C] + both[:, C:]


class Scan(NamedTuple):
    up_s: Any
    up_r: Any
    pre: Any
    x_s: Any
    x_r: Any
    down_s: Any
    down_r: Any


def groups_of(heads):
    return ((0,), tuple(range(1, heads)))


def kernel(heads, nx, ndp, ins, outs, local, info, scans, norm, gains, sems):
    q_hbm, k_hbm, v_hbm, o_hbm, log_hbm, gain_hbm, doc_hbm = ins
    gout, k_ref, v_ref, keyp_ref, valp_ref, end_tok_ref, *arriving = outs
    (
        (q_ref, o_ref, log_ref, gain_ref, doc_ref),
        (mask_ref, w_ref, u0_ref, qw_ref, open_ref),
        (part_ref, att_ref, ag_ref, bt1_ref),
    ) = local
    info_s, info_r, keep_ref, step_ref, reach_ref, end_ref, row_s, row_r = info
    st_s, st_r = norm
    g_s, g_r, h_s, h_r = gains
    load_sem, zs_sem, zr_sem, xs_sem, xr_sem, ds_sem, dr_sem = sems
    groups = groups_of(heads)
    ending_scans = [scan._replace(down_r=r) for scan, r in zip(scans[1], arriving)]
    scans = (scans[0], ending_scans)
    place = lax.axis_index("seq")
    me = lax.axis_index("dp")
    x = lax.div(place, NZ)
    z = lax.rem(place, NZ)
    rows = C // NZ
    tokens = 2 * C

    loads = [
        pltpu.make_async_copy(src, dst, load_sem.at[i])
        for i, (src, dst) in enumerate(
            (
                (log_hbm, log_ref),
                (doc_hbm, doc_ref),
                (k_hbm, k_ref),
                (v_hbm, v_ref),
                (q_hbm, q_ref),
                (o_hbm, o_ref),
                (gain_hbm, gain_ref.at[0]),
            )
        )
    ]
    for load in loads:
        load.start()

    aways = [NZ // 2] + [
        away for near in range(NZ // 2 - 1, 0, -1) for away in (near, NZ - near)
    ]
    z_peers = [lax.rem(z + away, NZ) for away in aways]
    x_peers = [lax.rem(x + away, nx) for away in range(1, nx)]
    dp_peers = [lax.rem(me + away, ndp) for away in range(1, ndp)]

    sent = []

    def exchange(peers, where, mine, count, source, slots, send_sem, recv_sem):
        for t in peers:
            pltpu.make_async_remote_copy(
                src_ref=source(t),
                dst_ref=slots.at[mine],
                send_sem=send_sem,
                recv_sem=recv_sem,
                device_id=where(t),
                device_id_type=MESH,
            ).start()
        slots[mine] = source(mine)[...]
        others = slots.at[pl.ds(0, count - 1)]
        whole = pltpu.make_async_remote_copy(
            src_ref=others,
            dst_ref=others,
            send_sem=send_sem,
            recv_sem=recv_sem,
            device_id=where(mine),
            device_id_type=MESH,
        )
        sent.append(whole)
        return whole.wait_recv

    def over_z(phase, source, slots):
        return exchange(
            z_peers,
            lambda t: {"seq": x * NZ + t},
            z,
            NZ,
            source,
            slots,
            zs_sem.at[phase],
            zr_sem.at[phase],
        )

    def over_x(phase, source, slots):
        return exchange(
            x_peers,
            lambda t: {"seq": t * NZ + z},
            x,
            nx,
            lambda t: source,
            slots,
            xs_sem.at[phase],
            xr_sem.at[phase],
        )

    barrier = pltpu.get_barrier_semaphore()

    def greet(**where):
        pl.semaphore_signal(barrier, inc=1, device_id=where, device_id_type=MESH)

    for t in z_peers:
        greet(seq=x * NZ + t)
    for t in x_peers:
        greet(seq=t * NZ + z)
    for t in dp_peers:
        greet(dp=t)

    for load in loads[:2]:
        load.wait()
    logs = jnp.concatenate(
        [log_ref[:, :C], log_ref[:, C:], jnp.zeros((8 - 2 * heads, C), F32)], axis=0
    )
    row_id = lax.broadcasted_iota(jnp.int32, (C, C), 0)
    col_id = lax.broadcasted_iota(jnp.int32, (C, C), 1)
    cum_rows = dot(logs, (row_id <= col_id).astype(F32), 1, 0, lax.Precision.HIGHEST)
    cum = cum_rows.T
    total = cum[C - 1 :, :]
    from_start = jnp.exp(cum)
    to_end = jnp.exp(total - cum)
    whole = jnp.exp(total)
    joined = jnp.where(doc_ref[0] == doc_ref[1], jnp.float32(1.0), jnp.float32(0.0))

    def at(table, block, head):
        r = block * heads + head
        return table[:, r : r + 1]

    def lanes(head):
        return slice(head * C, (head + 1) * C)

    lane = lax.broadcasted_iota(jnp.int32, (1, C), 1)
    line = jnp.zeros((1, C), F32)
    for head in range(heads):
        line = jnp.where(
            lane == head, at(whole, 0, head) * (joined * at(whole, 1, head)), line
        )
    for i in range(2):
        document = jnp.full((1, C), doc_ref[i], jnp.int32).astype(F32)
        line = jnp.where(lane == heads + i, document, line)
    info_s[...] = line

    for load in loads[2:4]:
        load.wait()
    for group, scan in zip(groups, scans[0]):
        for i, head in enumerate(group):
            updates = []
            for block in range(2):
                here = slice(block * C, (block + 1) * C)
                scaled = k_ref[here, lanes(head)].astype(F32) * at(to_end, block, head)
                updates.append(dot(scaled.astype(BF16), v_ref[here, lanes(head)], 0, 0))
            u0_ref[head] = updates[0]
            both = (joined * at(whole, 1, head)) * updates[0] + updates[1]
            scan.up_s[:, i] = both.reshape(NZ, rows, C)

    pl.semaphore_wait(barrier, (NZ - 1) + (nx - 1) + (ndp - 1))
    info_wait = over_z(0, lambda t: info_s, info_r)
    up_waits = [
        over_z(1 + g, lambda t, scan=scan: scan.up_s.at[t], scan.up_r)
        for g, scan in enumerate(scans[0])
    ]

    for load in loads[4:]:
        load.wait()
    for head in range(heads):
        for block in range(2):
            here = slice(block * C, (block + 1) * C)
            r = block * heads + head
            gap = cum[:, r : r + 1] - cum_rows[r : r + 1, :]
            mask = jnp.where(row_id >= col_id, jnp.exp(jnp.minimum(gap, 0.0)), 0.0)
            mask_ref[r] = mask
            query = q_ref[here, lanes(head)]
            key = k_ref[here, lanes(head)]
            value = v_ref[here, lanes(head)]
            weights = (dot(query, key, 1, 1) * mask).astype(BF16)
            w_ref[r] = weights
            near = dot(weights, value, 1, 0)
            opening = at(from_start, block, head)
            qw_ref[r] = (query.astype(F32) * opening).astype(BF16).T
            if block == 1:
                near = near + (joined * opening) * dot_split(query, u0_ref[head], 0)
                opening = opening * (joined * at(whole, 0, head))
            part_ref[here, lanes(head)] = near
            ending = at(to_end, block, head)
            if block == 0:
                ending = ending * (joined * at(whole, 1, head))
            open_ref[here, head : head + 1] = opening
            end_tok_ref[here, head : head + 1] = ending

    info_wait()

    def tile(line, i):
        return jnp.broadcast_to(line[:, i : i + 1], (rows, C))

    def goes_on(later, earlier):
        return jnp.where(
            later[:, heads : heads + 1] == earlier[:, heads + 1 : heads + 2], 1.0, 0.0
        )

    line = info_r[0]
    reach = jnp.ones((1, C), F32)
    for t in range(NZ):
        if t:
            earlier, line = line, info_r[t]
            keeps = goes_on(line, earlier)
            keep_ref[t] = jnp.broadcast_to(keeps, (rows, C))
            for head in range(heads):
                step_ref[0, t, head] = tile(keeps * earlier, head)
            reach = reach * (keeps * earlier)
        for head in range(heads):
            reach_ref[0, t, head] = tile(reach, head)
    first, last = info_r[0], info_r[NZ - 1]
    row_s[...] = jnp.where(
        lane < heads, reach * last, jnp.where(lane == heads, first, last)
    )
    row_wait = over_x(0, row_s, row_r)
    for head in range(heads):
        end_ref[0, head] = tile(last, head)
        end_ref[1, head] = tile(first, head)

    def row_lines_of():
        return [row_r[r] for r in range(nx)]

    def scan_row(back, scan, group):
        count = len(group)
        state = [jnp.zeros((rows, C), F32)] * count
        order = range(NZ - 1, -1, -1) if back else range(NZ)
        for t in order:
            for i in range(count):
                scan.pre[t, i] = state[i]
            if t != order[-1]:
                link = t if back else t + 1
                state = [
                    step_ref[back, link, head] * state[i] + keep_ref[link] * scan.up_r[t, i]
                    for i, head in enumerate(group)
                ]
            else:
                for i, head in enumerate(group):
                    scan.x_s[i] = end_ref[back, head] * state[i] + scan.up_r[t, i]

    def scan_rows(back, scan, group):
        count = len(group)
        row_lines = row_lines_of()
        entering = [jnp.zeros((rows, C), F32)] * count
        chosen = entering
        for r in range(nx - 2, -1, -1) if back else range(1, nx):
            other = r + 1 if back else r - 1
            keeps = goes_on(row_lines[max(r, other)], row_lines[min(r, other)])
            entering = [
                jnp.broadcast_to(keeps, (rows, C)) * scan.x_r[other, i]
                + tile(keeps * row_lines[other], head) * entering[i]
                for i, head in enumerate(group)
            ]
            chosen = [jnp.where(x == r, entering[i], chosen[i]) for i in range(count)]
        for t in range(NZ):
            for i, head in enumerate(group):
                scan.down_s[t, i] = scan.pre[t, i] + reach_ref[back, t, head] * chosen[i]

    def back_factors():
        reach = jnp.ones((1, C), F32)
        for t in range(NZ - 1, -1, -1):
            for head in range(heads):
                reach_ref[1, t, head] = tile(reach, head)
                if t:
                    step_ref[1, t, head] = keep_ref[t] * tile(info_r[t], head)
            if t:
                reach = reach * (goes_on(info_r[t], info_r[t - 1]) * info_r[t])

    def scan_all(back, up_waits):
        base = 1 + back * 2 * len(groups)
        x_waits, down_waits = [], []
        for g, (group, scan) in enumerate(zip(groups, scans[back])):
            up_waits[g]()
            scan_row(back, scan, group)
            x_waits.append(over_x(1 + back * len(groups) + g, scan.x_s, scan.x_r))
        if not back:
            row_wait()
        for g, (group, scan) in enumerate(zip(groups, scans[back])):
            x_waits[g]()
            scan_rows(back, scan, group)
            down_waits.append(
                over_z(
                    base + len(groups) + g, lambda t, scan=scan: scan.down_s.at[t], scan.down_r
                )
            )
        return down_waits

    down_waits = scan_all(0, up_waits)
    back_factors()

    squares = jnp.zeros((tokens, C), F32)
    inners = jnp.zeros((tokens, C), F32)
    for group, scan, arrived in zip(groups, scans[0], down_waits):
        arrived()
        for i, head in enumerate(group):
            came = scan.down_r[:, i].reshape(C, C)
            far = dot_split(q_ref[:, lanes(head)], came, 0)
            attention = part_ref[:, lanes(head)] + open_ref[:, head : head + 1] * far
            att_ref[:, lanes(head)] = attention
            wanted = o_ref[:, lanes(head)].astype(F32) * gain_ref[:, lanes(head)]
            squares = squares + attention * attention
            inners = inners + wanted * attention
    ones = jnp.ones((8, 2 * C), BF16)
    for i, summed in enumerate((squares, inners)):
        halves = jnp.concatenate(split(summed), axis=1)
        st_s[i : i + 1] = dot(ones, halves, 1, 1)[0:1]
    exchange(dp_peers, lambda t: {"dp": t}, me, ndp, lambda t: st_s, st_r, ds_sem, dr_sem)()
    sums = st_r[0]
    for r in range(1, ndp):
        sums = sums + st_r[r]
    means = sums / (ndp * heads * C)
    inverse = lax.rsqrt(means[0:1] + EPSILON)
    bend = means[1:2] * inverse * inverse
    side = lax.broadcasted_iota(jnp.int32, (8, tokens), 0)
    columns = jnp.where(side == 0, inverse, bend).T
    inverse = columns[:, 0:1]
    bend = columns[:, 1:2]

    up_waits = []
    for g, (group, scan) in enumerate(zip(groups, scans[1])):
        for i, head in enumerate(group):
            attention = att_ref[:, lanes(head)]
            wanted = o_ref[:, lanes(head)].astype(F32) * gain_ref[:, lanes(head)]
            grad = ((wanted - attention * bend) * inverse).astype(BF16)
            ag_ref[:, lanes(head)] = grad
            back = [
                dot(qw_ref[b * heads + head], grad[b * C : (b + 1) * C], 1, 0) for b in range(2)
            ]
            back_next = joined * back[1]
            bt1_ref[head] = back_next
            both = back[0] + at(whole, 0, head) * back_next
            scan.up_s[:, i] = both.reshape(NZ, rows, C)
        up_waits.append(
            over_z(
                1 + 2 * len(groups) + g, lambda t, scan=scan: scan.up_s.at[t], scan.up_r
            )
        )

    for head in range(heads):
        attention = att_ref[:, lanes(head)]
        out_cot = o_ref[:, lanes(head)].astype(F32)
        g_s[:, lanes(head)] = jnp.sum(out_cot * attention * inverse, axis=0, keepdims=True)
    gain_wait = over_z(1 + 4 * len(groups), lambda t: g_s, g_r)

    for head in range(heads):
        for block in range(2):
            here = slice(block * C, (block + 1) * C)
            r = block * heads + head
            grad = ag_ref[here, lanes(head)]
            value = v_ref[here, lanes(head)]
            key = k_ref[here, lanes(head)]
            value_part = dot(w_ref[r], grad, 0, 0)
            grad_weights = (dot(grad, value, 1, 1) * mask_ref[r]).astype(BF16)
            key_part = dot(grad_weights, q_ref[here, lanes(head)], 0, 0)
            if block == 0:
                ending = at(to_end, 0, head)
                key_part = key_part + ending * dot_split(value, bt1_ref[head], 1)
                value_part = value_part + ending * dot_split(key, bt1_ref[head], 0)
            keyp_ref[here, lanes(head)] = key_part
            valp_ref[here, lanes(head)] = value_part

    down_waits = scan_all(1, up_waits)

    gain_wait()
    row_gain = g_r[0]
    for t in range(1, NZ):
        row_gain = row_gain + g_r[t]
    h_s[...] = row_gain
    over_x(1 + 2 * len(groups), h_s, h_r)()
    gain = h_r[0]
    for r in range(1, nx):
        gain = gain + h_r[r]
    gout[...] = gain.reshape(heads * C)

    for arrived in down_waits:
        arrived()
    for copies in sent:
        copies.wait_send()


def finish(heads, ins, outs, scratch):
    gain_ref, k_ref, v_ref, keyp_ref, valp_ref, end_tok_ref, *arriving = ins
    kout_hbm, vout_hbm, gout_hbm = outs
    kout, vout, sem = scratch
    stores = [pltpu.make_async_copy(gain_ref, gout_hbm, sem.at[2 * heads])]
    stores[0].start()
    for group, down_r in zip(groups_of(heads), arriving):
        for i, head in enumerate(group):
            lanes = slice(head * C, (head + 1) * C)
            came = down_r[:, i].reshape(C, C)
            ending = end_tok_ref[:, head : head + 1]
            far = ending * dot_split(v_ref[:, lanes], came, 1)
            kout[:, lanes] = (keyp_ref[:, lanes] + far).astype(BF16)
            far = ending * dot_split(k_ref[:, lanes], came, 0)
            vout[:, lanes] = (valp_ref[:, lanes] + far).astype(BF16)
            for j, (src, dst) in enumerate(((kout, kout_hbm), (vout, vout_hbm))):
                store = pltpu.make_async_copy(
                    src.at[:, lanes], dst.at[:, lanes], sem.at[2 * head + j]
                )
                store.start()
                stores.append(store)
    for store in stores:
        store.wait()


def per_device(queries, keys, values, out_grad, log_decay, norm_gain, doc_ids):
    tokens, features = queries.shape
    heads = log_decay.shape[1]
    ndp = lax.axis_size("dp")
    nx = lax.axis_size("seq") // NZ
    rows = C // NZ
    groups = groups_of(heads)
    wide = (tokens, features)
    squares = (2 * heads, C, C)
    anywhere = pl.BlockSpec(memory_space=pl.ANY)
    vmem = pltpu.VMEM
    dma = pltpu.SemaphoreType.DMA
    local = (
        (
            vmem(wide, BF16),
            vmem(wide, BF16),
            vmem((heads, tokens), F32),
            vmem((1, features), F32),
            pltpu.SMEM((2,), jnp.int32),
        ),
        (
            vmem(squares, F32),
            vmem(squares, BF16),
            vmem((heads, C, C), F32),
            vmem(squares, BF16),
            vmem((tokens, heads), F32),
        ),
        (
            vmem(wide, F32),
            vmem(wide, F32),
            vmem(wide, BF16),
            vmem((heads, C, C), F32),
        ),
    )
    info = (
        vmem((1, C), F32),
        vmem((NZ, 1, C), F32),
        vmem((NZ, rows, C), F32),
        vmem((2, NZ, heads, rows, C), F32),
        vmem((2, NZ, heads, rows, C), F32),
        vmem((2, heads, rows, C), F32),
        vmem((1, C), F32),
        vmem((nx, 1, C), F32),
    )

    def scan_of(count):
        table = (NZ, count, rows, C)
        return Scan(
            up_s=vmem(table, F32),
            up_r=vmem(table, F32),
            pre=vmem(table, F32),
            x_s=vmem((count, rows, C), F32),
            x_r=vmem((nx, count, rows, C), F32),
            down_s=vmem(table, F32),
            down_r=vmem(table, F32),
        )

    scans = tuple(tuple(scan_of(len(group)) for group in groups) for _ in range(2))
    norm = (vmem((2, tokens), F32), vmem((ndp, 2, tokens), F32))
    gains = (
        vmem((1, features), F32),
        vmem((NZ, 1, features), F32),
        vmem((1, features), F32),
        vmem((nx, 1, features), F32),
    )
    z_count, x_count = 2 + 4 * len(groups), 2 + 2 * len(groups)
    sems = (
        dma((7,)),
        dma((z_count,)),
        dma((z_count,)),
        dma((x_count,)),
        dma((x_count,)),
        dma,
        dma,
    )
    between = (
        vmem((features,), F32),
        vmem(wide, BF16),
        vmem(wide, BF16),
        vmem(wide, F32),
        vmem(wide, F32),
        vmem((tokens, heads), F32),
    ) + tuple(vmem((NZ, len(group), rows, C), F32) for group in groups)
    scratch, tree = jax.tree.flatten((local, info, scans, norm, gains, sems))

    def body(*refs):
        ins, outs, rest = refs[:7], refs[7 : 7 + len(between)], refs[7 + len(between) :]
        kernel(heads, nx, ndp, ins, outs, *jax.tree.unflatten(tree, rest))

    def last(*refs):
        finish(heads, refs[: len(between)], refs[len(between) :][:3], refs[len(between) + 3 :])

    inside = pl.BlockSpec(memory_space=pltpu.VMEM)
    held = pl.pallas_call(
        body,
        out_shape=between,
        in_specs=[anywhere] * 7,
        out_specs=(inside,) * len(between),
        scratch_shapes=scratch,
        compiler_params=pltpu.CompilerParams(collective_id=0, has_side_effects=True),
        name="attention_core",
    )(queries, keys, values, out_grad, log_decay.T, norm_gain, doc_ids)
    return pl.pallas_call(
        last,
        out_shape=(
            jax.ShapeDtypeStruct(wide, BF16),
            jax.ShapeDtypeStruct(wide, BF16),
            jax.ShapeDtypeStruct((features,), F32),
        ),
        in_specs=[inside] * len(between),
        out_specs=(anywhere,) * 3,
        scratch_shapes=[vmem(wide, BF16), vmem(wide, BF16), dma((2 * heads + 1,))],
        name="outputs",
    )(*(pltpu.with_memory_space_constraint(part, pltpu.VMEM) for part in held))


def solution(mesh):
    placed = (
        P("seq", "dp"),
        P("seq", "dp"),
        P("seq", "dp"),
        P("seq", "dp"),
        P("seq", "dp"),
        P("dp"),
        P("seq"),
    )
    return jax.shard_map(
        per_device,
        mesh=mesh,
        in_specs=placed,
        out_specs=(P("seq", "dp"), P("seq", "dp"), P("dp")),
        check_vma=False,
    )
```

```python
from typing import Any, NamedTuple

import jax
import jax.numpy as jnp
from jax import lax
from jax.experimental import pallas as pl
from jax.experimental.pallas import tpu as pltpu
from jax.sharding import PartitionSpec as P

C = 128
NZ = 16
EPSILON = 1e-06
MESH = pl.DeviceIdType.MESH
F32 = jnp.float32
BF16 = jnp.bfloat16


def dot(a, b, ca, cb, precision=None):
    return lax.dot_general(
        a, b, (((ca,), (cb,)), ((), ())), precision=precision, preferred_element_type=F32
    )


def split(x):
    high = x.astype(BF16)
    return high, (x - high.astype(F32)).astype(BF16)


def dot_split(a, b, cb):
    high, low = split(b)
    both = dot(a, jnp.concatenate([high, low], axis=1 - cb), 1, cb)
    return both[:, :C] + both[:, C:]


class Scan(NamedTuple):
    up_s: Any
    up_r: Any
    pre: Any
    x_s: Any
    x_r: Any
    down_s: Any
    down_r: Any


def groups_of(heads):
    return ((0,), tuple(range(1, heads)))


def kernel(heads, nx, ndp, ins, outs, local, info, scans, norm, gains, sems):
    q_hbm, k_hbm, v_hbm, o_hbm, log_hbm, gain_hbm, doc_hbm = ins
    gout, k_ref, v_ref, keyp_ref, valp_ref, end_tok_ref, *arriving = outs
    (
        (q_ref, o_ref, log_ref, gain_ref, doc_ref),
        (mask_ref, w_ref, u0_ref, qw_ref, open_ref),
        (part_ref, att_ref, ag_ref, bt1_ref),
    ) = local
    info_s, info_r, keep_ref, step_ref, reach_ref, end_ref, row_s, row_r = info
    st_s, st_r = norm
    g_s, g_r, h_s, h_r = gains
    load_sem, zs_sem, zr_sem, xs_sem, xr_sem, ds_sem, dr_sem = sems
    groups = groups_of(heads)
    ending_scans = [scan._replace(down_r=r) for scan, r in zip(scans[1], arriving)]
    scans = (scans[0], ending_scans)
    place = lax.axis_index("seq")
    me = lax.axis_index("dp")
    x = lax.div(place, NZ)
    z = lax.rem(place, NZ)
    rows = C // NZ
    tokens = 2 * C

    def aways(count):
        return sorted(range(1, count), key=lambda away: (-min(away, count - away), -away))

    z_peers = [lax.rem(z + away, NZ) for away in aways(NZ)]
    x_peers = [lax.rem(x + away, nx) for away in aways(nx)]
    dp_peers = [lax.rem(me + away, ndp) for away in aways(ndp)]

    barrier = pltpu.get_barrier_semaphore()

    def greet(**where):
        pl.semaphore_signal(barrier, inc=1, device_id=where, device_id_type=MESH)

    for t in z_peers:
        greet(seq=x * NZ + t)
    for t in x_peers:
        greet(seq=t * NZ + z)
    for t in dp_peers:
        greet(dp=t)

    loads = [
        pltpu.make_async_copy(src, dst, load_sem.at[i])
        for i, (src, dst) in enumerate(
            (
                (log_hbm, log_ref),
                (doc_hbm, doc_ref),
                (k_hbm, k_ref),
                (v_hbm, v_ref),
                (q_hbm, q_ref),
                (o_hbm, o_ref),
                (gain_hbm, gain_ref.at[0]),
            )
        )
    ]
    for load in loads:
        load.start()

    sent = []

    def exchange(peers, where, mine, count, source, slots, send_sem, recv_sem):
        for t in peers:
            pltpu.make_async_remote_copy(
                src_ref=source(t),
                dst_ref=slots.at[mine],
                send_sem=send_sem,
                recv_sem=recv_sem,
                device_id=where(t),
                device_id_type=MESH,
            ).start()
        slots[mine] = source(mine)[...]
        others = slots.at[pl.ds(0, count - 1)]
        whole = pltpu.make_async_remote_copy(
            src_ref=others,
            dst_ref=others,
            send_sem=send_sem,
            recv_sem=recv_sem,
            device_id=where(mine),
            device_id_type=MESH,
        )
        sent.append(whole)
        return whole.wait_recv

    def over_z(phase, source, slots):
        return exchange(
            z_peers,
            lambda t: {"seq": x * NZ + t},
            z,
            NZ,
            source,
            slots,
            zs_sem.at[phase],
            zr_sem.at[phase],
        )

    def over_x(phase, source, slots):
        return exchange(
            x_peers,
            lambda t: {"seq": t * NZ + z},
            x,
            nx,
            lambda t: source,
            slots,
            xs_sem.at[phase],
            xr_sem.at[phase],
        )

    for load in loads[:2]:
        load.wait()
    logs = jnp.concatenate(
        [log_ref[:, :C], log_ref[:, C:], jnp.zeros((8 - 2 * heads, C), F32)], axis=0
    )
    row_id = lax.broadcasted_iota(jnp.int32, (C, C), 0)
    col_id = lax.broadcasted_iota(jnp.int32, (C, C), 1)
    cum_rows = dot(logs, (row_id <= col_id).astype(F32), 1, 0, lax.Precision.HIGHEST)
    cum = cum_rows.T
    total = cum[C - 1 :, :]
    from_start = jnp.exp(cum)
    to_end = jnp.exp(total - cum)
    whole = jnp.exp(total)
    joined = jnp.where(doc_ref[0] == doc_ref[1], jnp.float32(1.0), jnp.float32(0.0))

    def at(table, block, head):
        r = block * heads + head
        return table[:, r : r + 1]

    def lanes(head):
        return slice(head * C, (head + 1) * C)

    lane = lax.broadcasted_iota(jnp.int32, (1, C), 1)
    line = jnp.zeros((1, C), F32)
    for head in range(heads):
        line = jnp.where(
            lane == head, at(whole, 0, head) * (joined * at(whole, 1, head)), line
        )
    for i in range(2):
        document = jnp.full((1, C), doc_ref[i], jnp.int32).astype(F32)
        line = jnp.where(lane == heads + i, document, line)
    info_s[...] = line

    for load in loads[2:4]:
        load.wait()
    for group, scan in zip(groups, scans[0]):
        for i, head in enumerate(group):
            updates = []
            for block in range(2):
                here = slice(block * C, (block + 1) * C)
                scaled = k_ref[here, lanes(head)].astype(F32) * at(to_end, block, head)
                updates.append(dot(scaled.astype(BF16), v_ref[here, lanes(head)], 0, 0))
            u0_ref[head] = updates[0]
            both = (joined * at(whole, 1, head)) * updates[0] + updates[1]
            scan.up_s[:, i] = both.reshape(NZ, rows, C)

    pl.semaphore_wait(barrier, (NZ - 1) + (nx - 1) + (ndp - 1))
    info_wait = over_z(0, lambda t: info_s, info_r)
    up_waits = [
        over_z(1 + g, lambda t, scan=scan: scan.up_s.at[t], scan.up_r)
        for g, scan in enumerate(scans[0])
    ]

    for load in loads[4:]:
        load.wait()
    for head in range(heads):
        for block in range(2):
            here = slice(block * C, (block + 1) * C)
            r = block * heads + head
            gap = cum[:, r : r + 1] - cum_rows[r : r + 1, :]
            mask = jnp.where(row_id >= col_id, jnp.exp(jnp.minimum(gap, 0.0)), 0.0)
            mask_ref[r] = mask
            query = q_ref[here, lanes(head)]
            key = k_ref[here, lanes(head)]
            value = v_ref[here, lanes(head)]
            weights = (dot(query, key, 1, 1) * mask).astype(BF16)
            w_ref[r] = weights
            near = dot(weights, value, 1, 0)
            opening = at(from_start, block, head)
            qw_ref[r] = (query.astype(F32) * opening).astype(BF16).T
            if block == 1:
                near = near + (joined * opening) * dot_split(query, u0_ref[head], 0)
                opening = opening * (joined * at(whole, 0, head))
            part_ref[here, lanes(head)] = near
            ending = at(to_end, block, head)
            if block == 0:
                ending = ending * (joined * at(whole, 1, head))
            open_ref[here, head : head + 1] = opening
            end_tok_ref[here, head : head + 1] = ending

    info_wait()

    def tile(line, i):
        return jnp.broadcast_to(line[:, i : i + 1], (rows, C))

    def goes_on(later, earlier):
        return jnp.where(
            later[:, heads : heads + 1] == earlier[:, heads + 1 : heads + 2], 1.0, 0.0
        )

    line = info_r[0]
    reach = jnp.ones((1, C), F32)
    for t in range(NZ):
        if t:
            earlier, line = line, info_r[t]
            keeps = goes_on(line, earlier)
            keep_ref[t] = jnp.broadcast_to(keeps, (rows, C))
            for head in range(heads):
                step_ref[0, t, head] = tile(keeps * earlier, head)
            reach = reach * (keeps * earlier)
        for head in range(heads):
            reach_ref[0, t, head] = tile(reach, head)
    first, last = info_r[0], info_r[NZ - 1]
    row_s[...] = jnp.where(
        lane < heads, reach * last, jnp.where(lane == heads, first, last)
    )
    row_wait = over_x(0, row_s, row_r)
    for head in range(heads):
        end_ref[0, head] = tile(last, head)
        end_ref[1, head] = tile(first, head)

    def row_lines_of():
        return [row_r[r] for r in range(nx)]

    def scan_row(back, scan, group):
        count = len(group)
        state = [jnp.zeros((rows, C), F32)] * count
        order = range(NZ - 1, -1, -1) if back else range(NZ)
        for t in order:
            for i in range(count):
                scan.pre[t, i] = state[i]
            if t != order[-1]:
                link = t if back else t + 1
                state = [
                    step_ref[back, link, head] * state[i] + keep_ref[link] * scan.up_r[t, i]
                    for i, head in enumerate(group)
                ]
            else:
                for i, head in enumerate(group):
                    scan.x_s[i] = end_ref[back, head] * state[i] + scan.up_r[t, i]

    def scan_rows(back, scan, group):
        count = len(group)
        row_lines = row_lines_of()
        entering = [jnp.zeros((rows, C), F32)] * count
        chosen = entering
        for r in range(nx - 2, -1, -1) if back else range(1, nx):
            other = r + 1 if back else r - 1
            keeps = goes_on(row_lines[max(r, other)], row_lines[min(r, other)])
            entering = [
                jnp.broadcast_to(keeps, (rows, C)) * scan.x_r[other, i]
                + tile(keeps * row_lines[other], head) * entering[i]
                for i, head in enumerate(group)
            ]
            chosen = [jnp.where(x == r, entering[i], chosen[i]) for i in range(count)]
        for t in range(NZ):
            for i, head in enumerate(group):
                scan.down_s[t, i] = scan.pre[t, i] + reach_ref[back, t, head] * chosen[i]

    def back_factors():
        reach = jnp.ones((1, C), F32)
        for t in range(NZ - 1, -1, -1):
            for head in range(heads):
                reach_ref[1, t, head] = tile(reach, head)
                if t:
                    step_ref[1, t, head] = keep_ref[t] * tile(info_r[t], head)
            if t:
                reach = reach * (goes_on(info_r[t], info_r[t - 1]) * info_r[t])

    def scan_all(back, up_waits):
        base = 1 + back * 2 * len(groups)
        x_waits, down_waits = [], []
        for g, (group, scan) in enumerate(zip(groups, scans[back])):
            up_waits[g]()
            scan_row(back, scan, group)
            x_waits.append(over_x(1 + back * len(groups) + g, scan.x_s, scan.x_r))
        if not back:
            row_wait()
        for g, (group, scan) in enumerate(zip(groups, scans[back])):
            x_waits[g]()
            scan_rows(back, scan, group)
            down_waits.append(
                over_z(
                    base + len(groups) + g, lambda t, scan=scan: scan.down_s.at[t], scan.down_r
                )
            )
        return down_waits

    down_waits = scan_all(0, up_waits)
    back_factors()

    squares = jnp.zeros((tokens, C), F32)
    inners = jnp.zeros((tokens, C), F32)
    for group, scan, arrived in zip(groups, scans[0], down_waits):
        arrived()
        for i, head in enumerate(group):
            came = scan.down_r[:, i].reshape(C, C)
            far = dot_split(q_ref[:, lanes(head)], came, 0)
            attention = part_ref[:, lanes(head)] + open_ref[:, head : head + 1] * far
            att_ref[:, lanes(head)] = attention
            wanted = o_ref[:, lanes(head)].astype(F32) * gain_ref[:, lanes(head)]
            squares = squares + attention * attention
            inners = inners + wanted * attention
    ones = jnp.ones((8, 2 * C), BF16)
    for i, summed in enumerate((squares, inners)):
        halves = jnp.concatenate(split(summed), axis=1)
        st_s[i : i + 1] = dot(ones, halves, 1, 1)[0:1]
    exchange(dp_peers, lambda t: {"dp": t}, me, ndp, lambda t: st_s, st_r, ds_sem, dr_sem)()
    sums = st_r[0]
    for r in range(1, ndp):
        sums = sums + st_r[r]
    means = sums / (ndp * heads * C)
    inverse = lax.rsqrt(means[0:1] + EPSILON)
    bend = means[1:2] * inverse * inverse
    side = lax.broadcasted_iota(jnp.int32, (8, tokens), 0)
    columns = jnp.where(side == 0, inverse, bend).T
    inverse = columns[:, 0:1]
    bend = columns[:, 1:2]

    up_waits = []
    for g, (group, scan) in enumerate(zip(groups, scans[1])):
        for i, head in enumerate(group):
            attention = att_ref[:, lanes(head)]
            wanted = o_ref[:, lanes(head)].astype(F32) * gain_ref[:, lanes(head)]
            grad = ((wanted - attention * bend) * inverse).astype(BF16)
            ag_ref[:, lanes(head)] = grad
            back = [
                dot(qw_ref[b * heads + head], grad[b * C : (b + 1) * C], 1, 0) for b in range(2)
            ]
            back_next = joined * back[1]
            bt1_ref[head] = back_next
            both = back[0] + at(whole, 0, head) * back_next
            scan.up_s[:, i] = both.reshape(NZ, rows, C)
        up_waits.append(
            over_z(
                1 + 2 * len(groups) + g, lambda t, scan=scan: scan.up_s.at[t], scan.up_r
            )
        )

    for head in range(heads):
        attention = att_ref[:, lanes(head)]
        out_cot = o_ref[:, lanes(head)].astype(F32)
        g_s[:, lanes(head)] = jnp.sum(out_cot * attention * inverse, axis=0, keepdims=True)
    gain_wait = over_z(1 + 4 * len(groups), lambda t: g_s, g_r)

    for head in range(heads):
        for block in range(2):
            here = slice(block * C, (block + 1) * C)
            r = block * heads + head
            grad = ag_ref[here, lanes(head)]
            value = v_ref[here, lanes(head)]
            key = k_ref[here, lanes(head)]
            value_part = dot(w_ref[r], grad, 0, 0)
            grad_weights = (dot(grad, value, 1, 1) * mask_ref[r]).astype(BF16)
            key_part = dot(grad_weights, q_ref[here, lanes(head)], 0, 0)
            if block == 0:
                ending = at(to_end, 0, head)
                key_part = key_part + ending * dot_split(value, bt1_ref[head], 1)
                value_part = value_part + ending * dot_split(key, bt1_ref[head], 0)
            keyp_ref[here, lanes(head)] = key_part
            valp_ref[here, lanes(head)] = value_part

    down_waits = scan_all(1, up_waits)

    gain_wait()
    row_gain = g_r[0]
    for t in range(1, NZ):
        row_gain = row_gain + g_r[t]
    h_s[...] = row_gain
    over_x(1 + 2 * len(groups), h_s, h_r)()
    gain = h_r[0]
    for r in range(1, nx):
        gain = gain + h_r[r]
    gout[...] = gain.reshape(heads * C)

    for arrived in down_waits:
        arrived()
    for copies in sent:
        copies.wait_send()


def finish(heads, ins, outs, scratch):
    gain_ref, k_ref, v_ref, keyp_ref, valp_ref, end_tok_ref, *arriving = ins
    kout_hbm, vout_hbm, gout_hbm = outs
    kout, vout, sem = scratch
    stores = [pltpu.make_async_copy(gain_ref, gout_hbm, sem.at[2 * heads])]
    stores[0].start()
    for group, down_r in zip(groups_of(heads), arriving):
        for i, head in enumerate(group):
            lanes = slice(head * C, (head + 1) * C)
            came = down_r[:, i].reshape(C, C)
            ending = end_tok_ref[:, head : head + 1]
            far = ending * dot_split(v_ref[:, lanes], came, 1)
            kout[:, lanes] = (keyp_ref[:, lanes] + far).astype(BF16)
            far = ending * dot_split(k_ref[:, lanes], came, 0)
            vout[:, lanes] = (valp_ref[:, lanes] + far).astype(BF16)
            for j, (src, dst) in enumerate(((kout, kout_hbm), (vout, vout_hbm))):
                store = pltpu.make_async_copy(
                    src.at[:, lanes], dst.at[:, lanes], sem.at[2 * head + j]
                )
                store.start()
                stores.append(store)
    for store in stores:
        store.wait()


def per_device(queries, keys, values, out_grad, log_decay, norm_gain, doc_ids):
    tokens, features = queries.shape
    heads = log_decay.shape[1]
    ndp = lax.axis_size("dp")
    nx = lax.axis_size("seq") // NZ
    rows = C // NZ
    groups = groups_of(heads)
    wide = (tokens, features)
    squares = (2 * heads, C, C)
    anywhere = pl.BlockSpec(memory_space=pl.ANY)
    vmem = pltpu.VMEM
    dma = pltpu.SemaphoreType.DMA
    local = (
        (
            vmem(wide, BF16),
            vmem(wide, BF16),
            vmem((heads, tokens), F32),
            vmem((1, features), F32),
            pltpu.SMEM((2,), jnp.int32),
        ),
        (
            vmem(squares, F32),
            vmem(squares, BF16),
            vmem((heads, C, C), F32),
            vmem(squares, BF16),
            vmem((tokens, heads), F32),
        ),
        (
            vmem(wide, F32),
            vmem(wide, F32),
            vmem(wide, BF16),
            vmem((heads, C, C), F32),
        ),
    )
    info = (
        vmem((1, C), F32),
        vmem((NZ, 1, C), F32),
        vmem((NZ, rows, C), F32),
        vmem((2, NZ, heads, rows, C), F32),
        vmem((2, NZ, heads, rows, C), F32),
        vmem((2, heads, rows, C), F32),
        vmem((1, C), F32),
        vmem((nx, 1, C), F32),
    )

    def scan_of(count):
        table = (NZ, count, rows, C)
        return Scan(
            up_s=vmem(table, F32),
            up_r=vmem(table, F32),
            pre=vmem(table, F32),
            x_s=vmem((count, rows, C), F32),
            x_r=vmem((nx, count, rows, C), F32),
            down_s=vmem(table, F32),
            down_r=vmem(table, F32),
        )

    scans = tuple(tuple(scan_of(len(group)) for group in groups) for _ in range(2))
    norm = (vmem((2, tokens), F32), vmem((ndp, 2, tokens), F32))
    gains = (
        vmem((1, features), F32),
        vmem((NZ, 1, features), F32),
        vmem((1, features), F32),
        vmem((nx, 1, features), F32),
    )
    z_count, x_count = 2 + 4 * len(groups), 2 + 2 * len(groups)
    sems = (
        dma((7,)),
        dma((z_count,)),
        dma((z_count,)),
        dma((x_count,)),
        dma((x_count,)),
        dma,
        dma,
    )
    between = (
        vmem((features,), F32),
        vmem(wide, BF16),
        vmem(wide, BF16),
        vmem(wide, F32),
        vmem(wide, F32),
        vmem((tokens, heads), F32),
    ) + tuple(vmem((NZ, len(group), rows, C), F32) for group in groups)
    scratch, tree = jax.tree.flatten((local, info, scans, norm, gains, sems))

    def body(*refs):
        ins, outs, rest = refs[:7], refs[7 : 7 + len(between)], refs[7 + len(between) :]
        kernel(heads, nx, ndp, ins, outs, *jax.tree.unflatten(tree, rest))

    def last(*refs):
        finish(heads, refs[: len(between)], refs[len(between) :][:3], refs[len(between) + 3 :])

    inside = pl.BlockSpec(memory_space=pltpu.VMEM)
    held = pl.pallas_call(
        body,
        out_shape=between,
        in_specs=[anywhere] * 7,
        out_specs=(inside,) * len(between),
        scratch_shapes=scratch,
        compiler_params=pltpu.CompilerParams(collective_id=0, has_side_effects=True),
        name="attention_core",
    )(queries, keys, values, out_grad, log_decay.T, norm_gain, doc_ids)
    return pl.pallas_call(
        last,
        out_shape=(
            jax.ShapeDtypeStruct(wide, BF16),
            jax.ShapeDtypeStruct(wide, BF16),
            jax.ShapeDtypeStruct((features,), F32),
        ),
        in_specs=[inside] * len(between),
        out_specs=(anywhere,) * 3,
        scratch_shapes=[vmem(wide, BF16), vmem(wide, BF16), dma((2 * heads + 1,))],
        name="outputs",
    )(*(pltpu.with_memory_space_constraint(part, pltpu.VMEM) for part in held))


def solution(mesh):
    placed = (
        P("seq", "dp"),
        P("seq", "dp"),
        P("seq", "dp"),
        P("seq", "dp"),
        P("seq", "dp"),
        P("dp"),
        P("seq"),
    )
    return jax.shard_map(
        per_device,
        mesh=mesh,
        in_specs=placed,
        out_specs=(P("seq", "dp"), P("seq", "dp"), P("dp")),
        check_vma=False,
    )
```

```python
from typing import Any, NamedTuple

import jax
import jax.numpy as jnp
from jax import lax
from jax.experimental import pallas as pl
from jax.experimental.pallas import tpu as pltpu
from jax.sharding import PartitionSpec as P

C = 128
NZ = 16
EPSILON = 1e-06
MESH = pl.DeviceIdType.MESH
F32 = jnp.float32
BF16 = jnp.bfloat16


def dot(a, b, ca, cb, precision=None):
    return lax.dot_general(
        a, b, (((ca,), (cb,)), ((), ())), precision=precision, preferred_element_type=F32
    )


def split(x):
    high = x.astype(BF16)
    return high, (x - high.astype(F32)).astype(BF16)


def dot_split(a, b, cb):
    high, low = split(b)
    both = dot(a, jnp.concatenate([high, low], axis=1 - cb), 1, cb)
    return both[:, :C] + both[:, C:]


class Scan(NamedTuple):
    up_s: Any
    up_r: Any
    pre: Any
    x_s: Any
    x_r: Any
    down_s: Any
    down_r: Any


def groups_of(heads):
    return ((0,), tuple(range(1, heads)))


def kernel(heads, nx, ndp, ins, outs, local, info, scans, norm, gains, sems):
    q_hbm, k_hbm, v_hbm, o_hbm, log_hbm, gain_hbm, doc_hbm = ins
    gout, k_ref, v_ref, keyp_ref, valp_ref, end_tok_ref, *arriving = outs
    (
        (q_ref, o_ref, log_ref, gain_ref, doc_ref),
        (mask_ref, w_ref, u0_ref, qw_ref, open_ref),
        (part_ref, att_ref, ag_ref, bt1_ref),
    ) = local
    keep_ref, step_ref, reach_ref, end_ref, row_s, row_r = info
    st_s, st_r = norm
    g_s, g_r, h_s, h_r = gains
    load_sem, zs_sem, zr_sem, xs_sem, xr_sem, ds_sem, dr_sem = sems
    groups = groups_of(heads)
    ending_scans = [scan._replace(down_r=r) for scan, r in zip(scans[1], arriving)]
    scans = (scans[0], ending_scans)
    place = lax.axis_index("seq")
    me = lax.axis_index("dp")
    x = lax.div(place, NZ)
    z = lax.rem(place, NZ)
    rows = C // NZ
    tokens = 2 * C

    def aways(count):
        return sorted(range(1, count), key=lambda away: (-min(away, count - away), -away))

    z_peers = [lax.rem(z + away, NZ) for away in aways(NZ)]
    x_peers = [lax.rem(x + away, nx) for away in aways(nx)]
    dp_peers = [lax.rem(me + away, ndp) for away in aways(ndp)]

    barrier = pltpu.get_barrier_semaphore()

    def greet(**where):
        pl.semaphore_signal(barrier, inc=1, device_id=where, device_id_type=MESH)

    for t in z_peers:
        greet(seq=x * NZ + t)
    for t in x_peers:
        greet(seq=t * NZ + z)
    for t in dp_peers:
        greet(dp=t)

    loads = [
        pltpu.make_async_copy(src, dst, load_sem.at[i])
        for i, (src, dst) in enumerate(
            (
                (log_hbm, log_ref),
                (doc_hbm, doc_ref),
                (k_hbm, k_ref),
                (v_hbm, v_ref),
                (q_hbm, q_ref),
                (o_hbm, o_ref),
                (gain_hbm, gain_ref.at[0]),
            )
        )
    ]
    for load in loads:
        load.start()

    sent = []

    def exchange(peers, where, mine, count, source, slots, send_sem, recv_sem):
        used = pl.ds(0, source(mine).shape[0])

        for t in peers:
            pltpu.make_async_remote_copy(
                src_ref=source(t),
                dst_ref=slots.at[mine, used],
                send_sem=send_sem,
                recv_sem=recv_sem,
                device_id=where(t),
                device_id_type=MESH,
            ).start()
        slots[mine, used] = source(mine)[...]
        others = slots.at[pl.ds(0, count - 1), used]
        whole = pltpu.make_async_remote_copy(
            src_ref=others,
            dst_ref=others,
            send_sem=send_sem,
            recv_sem=recv_sem,
            device_id=where(mine),
            device_id_type=MESH,
        )
        sent.append(whole)
        return whole.wait_recv

    def over_z(phase, source, slots):
        return exchange(
            z_peers,
            lambda t: {"seq": x * NZ + t},
            z,
            NZ,
            source,
            slots,
            zs_sem.at[phase],
            zr_sem.at[phase],
        )

    def over_x(phase, source, slots):
        return exchange(
            x_peers,
            lambda t: {"seq": t * NZ + z},
            x,
            nx,
            lambda t: source,
            slots,
            xs_sem.at[phase],
            xr_sem.at[phase],
        )

    for load in loads[:2]:
        load.wait()
    logs = jnp.concatenate(
        [log_ref[:, :C], log_ref[:, C:], jnp.zeros((8 - 2 * heads, C), F32)], axis=0
    )
    row_id = lax.broadcasted_iota(jnp.int32, (C, C), 0)
    col_id = lax.broadcasted_iota(jnp.int32, (C, C), 1)
    cum_rows = dot(logs, (row_id <= col_id).astype(F32), 1, 0, lax.Precision.HIGHEST)
    cum = cum_rows.T
    total = cum[C - 1 :, :]
    from_start = jnp.exp(cum)
    to_end = jnp.exp(total - cum)
    whole = jnp.exp(total)
    joined = jnp.where(doc_ref[0] == doc_ref[1], jnp.float32(1.0), jnp.float32(0.0))

    def at(table, block, head):
        r = block * heads + head
        return table[:, r : r + 1]

    def lanes(head):
        return slice(head * C, (head + 1) * C)

    lane = lax.broadcasted_iota(jnp.int32, (1, C), 1)
    line = jnp.zeros((1, C), F32)
    for head in range(heads):
        line = jnp.where(
            lane == head, at(whole, 0, head) * (joined * at(whole, 1, head)), line
        )
    for i in range(2):
        document = jnp.full((1, C), doc_ref[i], jnp.int32).astype(F32)
        line = jnp.where(lane == heads + i, document, line)
    for t in range(NZ):
        scans[0][0].up_s[t, len(groups[0]) * rows : len(groups[0]) * rows + 1] = line

    for load in loads[2:4]:
        load.wait()
    for group, scan in zip(groups, scans[0]):
        for i, head in enumerate(group):
            updates = []
            for block in range(2):
                here = slice(block * C, (block + 1) * C)
                scaled = k_ref[here, lanes(head)].astype(F32) * at(to_end, block, head)
                updates.append(dot(scaled.astype(BF16), v_ref[here, lanes(head)], 0, 0))
            u0_ref[head] = updates[0]
            both = (joined * at(whole, 1, head)) * updates[0] + updates[1]
            scan.up_s[:, i * rows : (i + 1) * rows] = both.reshape(NZ, rows, C)

    pl.semaphore_wait(barrier, (NZ - 1) + (nx - 1) + (ndp - 1))
    up_waits = [
        over_z(
            1 + g,
            lambda t, scan=scan, used=len(group) * rows + (g == 0): scan.up_s.at[
                t, pl.ds(0, used)
            ],
            scan.up_r,
        )
        for g, (group, scan) in enumerate(zip(groups, scans[0]))
    ]

    for load in loads[4:]:
        load.wait()
    for head in range(heads):
        for block in range(2):
            here = slice(block * C, (block + 1) * C)
            r = block * heads + head
            gap = cum[:, r : r + 1] - cum_rows[r : r + 1, :]
            mask = jnp.where(row_id >= col_id, jnp.exp(jnp.minimum(gap, 0.0)), 0.0)
            mask_ref[r] = mask
            query = q_ref[here, lanes(head)]
            key = k_ref[here, lanes(head)]
            value = v_ref[here, lanes(head)]
            weights = (dot(query, key, 1, 1) * mask).astype(BF16)
            w_ref[r] = weights
            near = dot(weights, value, 1, 0)
            opening = at(from_start, block, head)
            qw_ref[r] = (query.astype(F32) * opening).astype(BF16).T
            if block == 1:
                near = near + (joined * opening) * dot_split(query, u0_ref[head], 0)
                opening = opening * (joined * at(whole, 0, head))
            part_ref[here, lanes(head)] = near
            ending = at(to_end, block, head)
            if block == 0:
                ending = ending * (joined * at(whole, 1, head))
            open_ref[here, head : head + 1] = opening
            end_tok_ref[here, head : head + 1] = ending

    up_waits[0]()

    def info_of(t):
        row = len(groups[0]) * rows
        return scans[0][0].up_r[t, row : row + 1]

    def tile(line, i):
        return jnp.broadcast_to(line[:, i : i + 1], (rows, C))

    def goes_on(later, earlier):
        return jnp.where(
            later[:, heads : heads + 1] == earlier[:, heads + 1 : heads + 2], 1.0, 0.0
        )

    line = info_of(0)
    reach = jnp.ones((1, C), F32)
    for t in range(NZ):
        if t:
            earlier, line = line, info_of(t)
            keeps = goes_on(line, earlier)
            keep_ref[t] = jnp.broadcast_to(keeps, (rows, C))
            for head in range(heads):
                step_ref[0, t, head] = tile(keeps * earlier, head)
            reach = reach * (keeps * earlier)
        for head in range(heads):
            reach_ref[0, t, head] = tile(reach, head)
    first, last = info_of(0), info_of(NZ - 1)
    row_s[...] = jnp.where(
        lane < heads, reach * last, jnp.where(lane == heads, first, last)
    )
    row_wait = over_x(0, row_s, row_r)
    for head in range(heads):
        end_ref[0, head] = tile(last, head)
        end_ref[1, head] = tile(first, head)

    def row_lines_of():
        return [row_r[r] for r in range(nx)]

    def scan_row(back, scan, group):
        count = len(group)
        state = [jnp.zeros((rows, C), F32)] * count
        order = range(NZ - 1, -1, -1) if back else range(NZ)
        for t in order:
            for i in range(count):
                scan.pre[t, i] = state[i]
            if t != order[-1]:
                link = t if back else t + 1
                state = [
                    step_ref[back, link, head] * state[i] + keep_ref[link] * scan.up_r[t, i * rows : (i + 1) * rows]
                    for i, head in enumerate(group)
                ]
            else:
                for i, head in enumerate(group):
                    scan.x_s[i] = end_ref[back, head] * state[i] + scan.up_r[
                        t, i * rows : (i + 1) * rows
                    ]

    def scan_rows(back, scan, group):
        count = len(group)
        row_lines = row_lines_of()
        entering = [jnp.zeros((rows, C), F32)] * count
        chosen = entering
        for r in range(nx - 2, -1, -1) if back else range(1, nx):
            other = r + 1 if back else r - 1
            keeps = goes_on(row_lines[max(r, other)], row_lines[min(r, other)])
            entering = [
                jnp.broadcast_to(keeps, (rows, C)) * scan.x_r[other, i]
                + tile(keeps * row_lines[other], head) * entering[i]
                for i, head in enumerate(group)
            ]
            chosen = [jnp.where(x == r, entering[i], chosen[i]) for i in range(count)]
        for t in range(NZ):
            for i, head in enumerate(group):
                scan.down_s[t, i] = scan.pre[t, i] + reach_ref[back, t, head] * chosen[i]

    def back_factors():
        reach = jnp.ones((1, C), F32)
        for t in range(NZ - 1, -1, -1):
            for head in range(heads):
                reach_ref[1, t, head] = tile(reach, head)
                if t:
                    step_ref[1, t, head] = keep_ref[t] * tile(info_of(t), head)
            if t:
                reach = reach * (goes_on(info_of(t), info_of(t - 1)) * info_of(t))

    def scan_all(back, up_waits):
        base = 1 + back * 2 * len(groups)
        x_waits, down_waits = [], []
        for g, (group, scan) in enumerate(zip(groups, scans[back])):
            if back or g:
                up_waits[g]()
            scan_row(back, scan, group)
            x_waits.append(over_x(1 + back * len(groups) + g, scan.x_s, scan.x_r))
        if not back:
            row_wait()
        for g, (group, scan) in enumerate(zip(groups, scans[back])):
            x_waits[g]()
            scan_rows(back, scan, group)
            down_waits.append(
                over_z(
                    base + len(groups) + g, lambda t, scan=scan: scan.down_s.at[t], scan.down_r
                )
            )
        return down_waits

    down_waits = scan_all(0, up_waits)
    back_factors()

    squares = jnp.zeros((tokens, C), F32)
    inners = jnp.zeros((tokens, C), F32)
    for group, scan, arrived in zip(groups, scans[0], down_waits):
        arrived()
        for i, head in enumerate(group):
            came = scan.down_r[:, i].reshape(C, C)
            far = dot_split(q_ref[:, lanes(head)], came, 0)
            attention = part_ref[:, lanes(head)] + open_ref[:, head : head + 1] * far
            att_ref[:, lanes(head)] = attention
            wanted = o_ref[:, lanes(head)].astype(F32) * gain_ref[:, lanes(head)]
            squares = squares + attention * attention
            inners = inners + wanted * attention
    ones = jnp.ones((8, 2 * C), BF16)
    for i, summed in enumerate((squares, inners)):
        halves = jnp.concatenate(split(summed), axis=1)
        st_s[i : i + 1] = dot(ones, halves, 1, 1)[0:1]
    exchange(dp_peers, lambda t: {"dp": t}, me, ndp, lambda t: st_s, st_r, ds_sem, dr_sem)()
    sums = st_r[0]
    for r in range(1, ndp):
        sums = sums + st_r[r]
    means = sums / (ndp * heads * C)
    inverse = lax.rsqrt(means[0:1] + EPSILON)
    bend = means[1:2] * inverse * inverse
    side = lax.broadcasted_iota(jnp.int32, (8, tokens), 0)
    columns = jnp.where(side == 0, inverse, bend).T
    inverse = columns[:, 0:1]
    bend = columns[:, 1:2]

    up_waits = []
    for g, (group, scan) in enumerate(zip(groups, scans[1])):
        for i, head in enumerate(group):
            attention = att_ref[:, lanes(head)]
            wanted = o_ref[:, lanes(head)].astype(F32) * gain_ref[:, lanes(head)]
            grad = ((wanted - attention * bend) * inverse).astype(BF16)
            ag_ref[:, lanes(head)] = grad
            back = [
                dot(qw_ref[b * heads + head], grad[b * C : (b + 1) * C], 1, 0) for b in range(2)
            ]
            back_next = joined * back[1]
            bt1_ref[head] = back_next
            both = back[0] + at(whole, 0, head) * back_next
            scan.up_s[:, i * rows : (i + 1) * rows] = both.reshape(NZ, rows, C)
        up_waits.append(
            over_z(
                1 + 2 * len(groups) + g, lambda t, scan=scan: scan.up_s.at[t], scan.up_r
            )
        )

    for head in range(heads):
        attention = att_ref[:, lanes(head)]
        out_cot = o_ref[:, lanes(head)].astype(F32)
        g_s[:, lanes(head)] = jnp.sum(out_cot * attention * inverse, axis=0, keepdims=True)
    gain_wait = over_z(1 + 4 * len(groups), lambda t: g_s, g_r)

    for head in range(heads):
        for block in range(2):
            here = slice(block * C, (block + 1) * C)
            r = block * heads + head
            grad = ag_ref[here, lanes(head)]
            value = v_ref[here, lanes(head)]
            key = k_ref[here, lanes(head)]
            value_part = dot(w_ref[r], grad, 0, 0)
            grad_weights = (dot(grad, value, 1, 1) * mask_ref[r]).astype(BF16)
            key_part = dot(grad_weights, q_ref[here, lanes(head)], 0, 0)
            if block == 0:
                ending = at(to_end, 0, head)
                key_part = key_part + ending * dot_split(value, bt1_ref[head], 1)
                value_part = value_part + ending * dot_split(key, bt1_ref[head], 0)
            keyp_ref[here, lanes(head)] = key_part
            valp_ref[here, lanes(head)] = value_part

    down_waits = scan_all(1, up_waits)

    gain_wait()
    row_gain = g_r[0]
    for t in range(1, NZ):
        row_gain = row_gain + g_r[t]
    h_s[...] = row_gain
    over_x(1 + 2 * len(groups), h_s, h_r)()
    gain = h_r[0]
    for r in range(1, nx):
        gain = gain + h_r[r]
    gout[...] = gain.reshape(heads * C)

    for arrived in down_waits:
        arrived()
    for copies in sent:
        copies.wait_send()


def finish(heads, ins, outs, scratch):
    gain_ref, k_ref, v_ref, keyp_ref, valp_ref, end_tok_ref, *arriving = ins
    kout_hbm, vout_hbm, gout_hbm = outs
    kout, vout, sem = scratch
    stores = [pltpu.make_async_copy(gain_ref, gout_hbm, sem.at[2 * heads])]
    stores[0].start()
    for group, down_r in zip(groups_of(heads), arriving):
        for i, head in enumerate(group):
            lanes = slice(head * C, (head + 1) * C)
            came = down_r[:, i].reshape(C, C)
            ending = end_tok_ref[:, head : head + 1]
            far = ending * dot_split(v_ref[:, lanes], came, 1)
            kout[:, lanes] = (keyp_ref[:, lanes] + far).astype(BF16)
            far = ending * dot_split(k_ref[:, lanes], came, 0)
            vout[:, lanes] = (valp_ref[:, lanes] + far).astype(BF16)
            for j, (src, dst) in enumerate(((kout, kout_hbm), (vout, vout_hbm))):
                store = pltpu.make_async_copy(
                    src.at[:, lanes], dst.at[:, lanes], sem.at[2 * head + j]
                )
                store.start()
                stores.append(store)
    for store in stores:
        store.wait()


def per_device(queries, keys, values, out_grad, log_decay, norm_gain, doc_ids):
    tokens, features = queries.shape
    heads = log_decay.shape[1]
    ndp = lax.axis_size("dp")
    nx = lax.axis_size("seq") // NZ
    rows = C // NZ
    groups = groups_of(heads)
    wide = (tokens, features)
    squares = (2 * heads, C, C)
    anywhere = pl.BlockSpec(memory_space=pl.ANY)
    vmem = pltpu.VMEM
    dma = pltpu.SemaphoreType.DMA
    local = (
        (
            vmem(wide, BF16),
            vmem(wide, BF16),
            vmem((heads, tokens), F32),
            vmem((1, features), F32),
            pltpu.SMEM((2,), jnp.int32),
        ),
        (
            vmem(squares, F32),
            vmem(squares, BF16),
            vmem((heads, C, C), F32),
            vmem(squares, BF16),
            vmem((tokens, heads), F32),
        ),
        (
            vmem(wide, F32),
            vmem(wide, F32),
            vmem(wide, BF16),
            vmem((heads, C, C), F32),
        ),
    )
    info = (
        vmem((NZ, rows, C), F32),
        vmem((2, NZ, heads, rows, C), F32),
        vmem((2, NZ, heads, rows, C), F32),
        vmem((2, heads, rows, C), F32),
        vmem((1, C), F32),
        vmem((nx, 1, C), F32),
    )

    def scan_of(count, extra):
        table = (NZ, count, rows, C)
        taken = (NZ, count * rows + extra, C)
        return Scan(
            up_s=vmem(taken, F32),
            up_r=vmem(taken, F32),
            pre=vmem(table, F32),
            x_s=vmem((count, rows, C), F32),
            x_r=vmem((nx, count, rows, C), F32),
            down_s=vmem(table, F32),
            down_r=vmem(table, F32),
        )

    scans = tuple(
        tuple(
            scan_of(len(group), 8 if back == g == 0 else 0) for g, group in enumerate(groups)
        )
        for back in range(2)
    )
    norm = (vmem((2, tokens), F32), vmem((ndp, 2, tokens), F32))
    gains = (
        vmem((1, features), F32),
        vmem((NZ, 1, features), F32),
        vmem((1, features), F32),
        vmem((nx, 1, features), F32),
    )
    z_count, x_count = 2 + 4 * len(groups), 2 + 2 * len(groups)
    sems = (
        dma((7,)),
        dma((z_count,)),
        dma((z_count,)),
        dma((x_count,)),
        dma((x_count,)),
        dma,
        dma,
    )
    between = (
        vmem((features,), F32),
        vmem(wide, BF16),
        vmem(wide, BF16),
        vmem(wide, F32),
        vmem(wide, F32),
        vmem((tokens, heads), F32),
    ) + tuple(vmem((NZ, len(group), rows, C), F32) for group in groups)
    scratch, tree = jax.tree.flatten((local, info, scans, norm, gains, sems))

    def body(*refs):
        ins, outs, rest = refs[:7], refs[7 : 7 + len(between)], refs[7 + len(between) :]
        kernel(heads, nx, ndp, ins, outs, *jax.tree.unflatten(tree, rest))

    def last(*refs):
        finish(heads, refs[: len(between)], refs[len(between) :][:3], refs[len(between) + 3 :])

    inside = pl.BlockSpec(memory_space=pltpu.VMEM)
    held = pl.pallas_call(
        body,
        out_shape=between,
        in_specs=[anywhere] * 7,
        out_specs=(inside,) * len(between),
        scratch_shapes=scratch,
        compiler_params=pltpu.CompilerParams(collective_id=0, has_side_effects=True),
        name="attention_core",
    )(queries, keys, values, out_grad, log_decay.T, norm_gain, doc_ids)
    return pl.pallas_call(
        last,
        out_shape=(
            jax.ShapeDtypeStruct(wide, BF16),
            jax.ShapeDtypeStruct(wide, BF16),
            jax.ShapeDtypeStruct((features,), F32),
        ),
        in_specs=[inside] * len(between),
        out_specs=(anywhere,) * 3,
        scratch_shapes=[vmem(wide, BF16), vmem(wide, BF16), dma((2 * heads + 1,))],
        name="outputs",
    )(*(pltpu.with_memory_space_constraint(part, pltpu.VMEM) for part in held))


def solution(mesh):
    placed = (
        P("seq", "dp"),
        P("seq", "dp"),
        P("seq", "dp"),
        P("seq", "dp"),
        P("seq", "dp"),
        P("dp"),
        P("seq"),
    )
    return jax.shard_map(
        per_device,
        mesh=mesh,
        in_specs=placed,
        out_specs=(P("seq", "dp"), P("seq", "dp"), P("dp")),
        check_vma=False,
    )
```
